1024 devices in a mesh: segment: 4 (over x_lo), dp: 64 (over y, z), tensor: 4 (over x_hi, core).
Axes of the slice: x: 8 (x_hi: 2, x_lo: 4; x = x_hi * 4 + x_lo), y: 8, z: 8, core: 2. Of those that a mesh axis runs over, the one named last changes fastest.
Arguments:
- queries: bfloat16 [4, 16384, 1536], P('segment', 'dp', 'tensor'), as said below
- context: bfloat16 [4, 2, 16384, 1536], P('segment', None, 'dp', 'tensor'), as said below
- vis_blocks: int32 [4, 128, 2], P('segment', 'dp'), may hold values from 0 to 1, all different within a row
- vis_count: int32 [4, 128], P('segment', 'dp'), may hold values from 1 to 2
- w_out: bfloat16 [4, 1536, 1536], P('segment', 'dp', 'tensor'), may hold values from -0.15625 to 0.15625
- grad_out: bfloat16 [4, 16384, 1536], P('segment', 'dp'), may hold values from -16 to 16
Outputs:
- grad_queries: bfloat16 [4, 16384, 1536], P('segment', 'dp', 'tensor')
- grad_context: bfloat16 [4, 2, 16384, 1536], P('segment', None, 'dp', 'tensor')
- grad_w_out: float32 [4, 1536, 1536], P('segment', 'dp', 'tensor')
The draws below stay inside these ranges and needn't reach their ends.
Inputs may be any that keep to these rules, and one draw needn't show every extreme that they name: `vis_blocks`: each row names 2 different context blocks of its scene. `queries`: entries lie within -5 and 5. `context`: entries lie within -5 and 5.
All inputs are finite; a program needn't handle non-finite values.
Results may differ from the reference program's by a relative error of at most 0.034.
Values may be sent and summed in bfloat16 or wider, within the bound.
No kernel may reach another device: no remote copies, remote signals or barrier semaphores. Data moves between devices by JAX's collectives and lax.ppermute only.
A program may use at most 32 MiB of HBM per device.

```python
import jax
import jax.numpy as jnp
from jax import lax

D = 1536
HD = 128
BLK = 128
CTX_BLK = 2
VIS = 2
TOK_DEV = 256
TOKENS = 16384
QB = 2
QBLOCKS = 128
CTX = 16384
HF = 1536
N_SEGMENT = 4
N_DP = 64


def draw_queries(key, part):
    base = jnp.clip(jax.random.normal(jax.random.fold_in(key, 1), (N_SEGMENT, TOKENS, HF), jnp.float32), -4.0, 4.0)
    return base.astype(jnp.bfloat16)


def draw_context(key, part):
    base = jnp.clip(jax.random.normal(jax.random.fold_in(key, 3), (N_SEGMENT, 2, CTX, HF), jnp.float32), -4.0, 4.0)
    return base.astype(jnp.bfloat16)


def with_ends(array, rng, smallest, top_value):
    shape = array.shape
    index_at = [jax.random.randint(jax.random.fold_in(rng, axis), (), 0, shape[axis]) for axis in range(len(shape))]
    array = array.at[tuple(index_at)].set(smallest)
    longest = shape.index(max(shape))
    index_at[longest] = (index_at[longest] + 1) % shape[longest]
    return array.at[tuple(index_at)].set(top_value)


def strengthened(array, stream_key, source, target, parts, factor):
    owner, partner = [(jnp.arange(array.shape[axis_at]) // (array.shape[axis_at] // parts)).reshape([-1 if axis == axis_at else 1 for axis in range(array.ndim)]) for axis_at in (source, target)]
    chosen = jax.random.permutation(stream_key, parts)[partner]
    strong = (owner == chosen) | (owner == (partner + parts // 2) % parts)
    return jnp.where(strong, factor * array, array)


def levels(key, shape, pieces, smallest, largest):
    def one(axis_at, blocks):
        steps = jax.random.uniform(jax.random.fold_in(jax.random.fold_in(key, 6), axis_at), (blocks,), jnp.float32, smallest / len(pieces), largest / len(pieces))
        return jnp.repeat(jnp.exp(steps), shape[axis_at] // blocks).reshape((-1,) + (1,) * (len(shape) - axis_at - 1))

    level = one(*pieces[0])
    for cut in pieces[1:]:
        level = level * one(*cut)
    return level


def choose_distinct(rng, rows, amount, top, lift):
    order = jax.random.permutation(jax.random.fold_in(rng, 1), amount)
    favour = order
    for power in range(3):
        favour = favour * favour // amount
    favour = favour * lift // amount
    lots = jax.random.randint(jax.random.fold_in(rng, 2), (rows, amount), 0, 4096) + favour
    holders = jax.random.permutation(jax.random.fold_in(rng, 3), rows)[jnp.arange(amount) % rows]
    lots = jnp.where(jnp.arange(rows)[:, None] == holders[None, :], 1 << 14, lots)
    score = lots * amount + jnp.arange(amount)
    return lax.top_k(score.astype(jnp.int32), top)[1].astype(jnp.int32)


def gaussian(key, dims, spread, bound, cuts=(), kind=jnp.bfloat16):
    entries = spread * jax.random.normal(key, dims, jnp.float32)
    if cuts:
        entries = entries * levels(key, dims, cuts, -0.22, 0.18)
    return jnp.clip(entries, -bound, bound).astype(kind)


def gaussian_with(rng, dims, width, bound, cuts, heavy, kind=jnp.bfloat16):
    values = width * jax.random.normal(rng, dims, jnp.float32)
    if cuts:
        values = values * levels(rng, dims, cuts, -0.22, 0.18)
    return jnp.clip(strengthened(values, jax.random.fold_in(rng, 3), *heavy), -bound, bound).astype(kind)


def setup_inputs(seed: int = 0) -> dict:
    splits = jax.random.split(jax.random.key(seed), 7)
    queries = draw_queries(jax.random.fold_in(splits[6], 71), 0)
    context = draw_context(jax.random.fold_in(splits[6], 71), 0)
    vis_blocks = choose_distinct(splits[2], N_SEGMENT * QBLOCKS, CTX_BLK, VIS, 0).reshape((N_SEGMENT, QBLOCKS, VIS))
    vis_count = with_ends(jax.random.randint(splits[3], (N_SEGMENT, QBLOCKS), 1, VIS + 1), jax.random.fold_in(splits[3], 1), 1, VIS).astype(jnp.int32)
    w_out = gaussian(splits[4], (N_SEGMENT, D, HF), HF ** -0.5, 0.15625, ((0, 4), (1, 64), (2, 4)))
    grad_out = gaussian_with(splits[5], (N_SEGMENT, TOKENS, D), 1.0, 16.0, ((0, 4), (1, 64)), (1, 2, 64, 4.0))
    return {"queries": queries, "context": context, "vis_blocks": vis_blocks, "vis_count": vis_count, "w_out": w_out, "grad_out": grad_out}


def scene_grads(queries, context, vis_blocks, vis_count, w_out, grad_out, index):
    segment_id = index // N_DP
    scene_id = index % N_DP
    before = (segment_id + N_SEGMENT - 1) % N_SEGMENT
    heads = HF // HD
    zero = jnp.zeros((), jnp.int32)
    qry = lax.dynamic_slice(queries, (segment_id, scene_id * TOK_DEV, zero), (1, TOK_DEV, HF))[0]
    pairs = lax.dynamic_slice(context, (before, zero, scene_id * CTX_BLK * BLK, zero), (1, 2, CTX_BLK * BLK, HF))[0]
    ids = lax.dynamic_slice(vis_blocks, (segment_id, scene_id * QB, zero), (1, QB, VIS))[0]
    cnt = lax.dynamic_slice(vis_count, (segment_id, scene_id * QB), (1, QB))[0]
    weight = lax.dynamic_slice(w_out, (segment_id, zero, zero), (1, D, HF))[0]
    cotan = lax.dynamic_slice(grad_out, (segment_id, scene_id * TOK_DEV, zero), (1, TOK_DEV, D))[0]
    scale = 1.0 / (HD ** 0.5)
    qf = qry.reshape(QB, BLK, heads, HD).astype(jnp.float32)
    keys_all = pairs[0].reshape(CTX_BLK, BLK, heads, HD)
    vals_all = pairs[1].reshape(CTX_BLK, BLK, heads, HD)
    keys = keys_all[ids].astype(jnp.float32)
    vals = vals_all[ids].astype(jnp.float32)
    score = jnp.einsum('qihd,qvjhd->qhivj', qf, keys) * scale
    live = jnp.arange(VIS)[None, :] < cnt[:, None]
    score = jnp.where(live[:, None, None, :, None], score, jnp.float32(-1e30))
    top = jnp.max(score, axis=(3, 4), keepdims=True)
    expo = jnp.exp(score - top)
    prob = expo / jnp.sum(expo, axis=(3, 4), keepdims=True)
    prob_b = prob.astype(jnp.bfloat16)
    attn = jnp.einsum('qhivj,qvjhd->qihd', prob_b.astype(jnp.float32), vals).astype(jnp.bfloat16)
    d_attn = jnp.dot(cotan, weight, preferred_element_type=jnp.float32).astype(jnp.bfloat16)
    da4 = d_attn.reshape(QB, BLK, heads, HD).astype(jnp.float32)
    delta = jnp.sum(da4 * attn.astype(jnp.float32), axis=-1).transpose(0, 2, 1)
    dprob = jnp.einsum('qihd,qvjhd->qhivj', da4, vals)
    dscore = (prob * (dprob - delta[:, :, :, None, None])).astype(jnp.bfloat16).astype(jnp.float32)
    grad_q = (jnp.einsum('qhivj,qvjhd->qihd', dscore, keys) * scale).astype(jnp.bfloat16)
    dkey = jnp.einsum('qhivj,qihd->qvjhd', dscore, qf) * scale
    dval = jnp.einsum('qhivj,qihd->qvjhd', prob_b.astype(jnp.float32), da4)
    onehot = (ids.reshape(-1)[:, None] == jnp.arange(CTX_BLK)[None, :]).astype(jnp.float32)
    gk = jnp.einsum('sc,sjhd->cjhd', onehot, dkey.reshape(QB * VIS, BLK, heads, HD), precision=lax.Precision.HIGHEST)
    gv = jnp.einsum('sc,sjhd->cjhd', onehot, dval.reshape(QB * VIS, BLK, heads, HD), precision=lax.Precision.HIGHEST)
    grad_kv = jnp.stack([gk, gv]).reshape(2, CTX_BLK * BLK, HF).astype(jnp.bfloat16)
    return grad_q.reshape(TOK_DEV, HF), grad_kv, attn.reshape(TOK_DEV, HF)


def reference(queries, context, vis_blocks, vis_count, w_out, grad_out):
    def one(index):
        return scene_grads(queries, context, vis_blocks, vis_count, w_out, grad_out, index)

    grad_q, grad_kv, attn = lax.map(one, jnp.arange(N_SEGMENT * N_DP, dtype=jnp.int32))
    grad_queries = grad_q.reshape(N_SEGMENT, TOKENS, HF)
    grad_used = grad_kv.reshape(N_SEGMENT, N_DP, 2, CTX_BLK * BLK, HF).transpose(0, 2, 1, 3, 4).reshape(N_SEGMENT, 2, CTX, HF)
    grad_context = jnp.roll(grad_used, -1, axis=0)
    attn_all = attn.reshape(N_SEGMENT, N_DP, TOK_DEV, HF)
    cotan_all = grad_out.reshape(N_SEGMENT, N_DP, TOK_DEV, D)

    def weight_term(index):
        def add_scene(total, pair):
            cot, act = pair
            term = lax.dot_general(cot, act, (((0,), (0,)), ((), ())), preferred_element_type=jnp.float32)
            return total + term, None

        total, unused = lax.scan(add_scene, jnp.zeros((D, HF), jnp.float32), (cotan_all[index], attn_all[index]))
        return total

    grad_w_out = lax.map(weight_term, jnp.arange(N_SEGMENT, dtype=jnp.int32))
    return grad_queries, grad_context, grad_w_out
```

```python
import jax
import jax.numpy as jnp
from jax import lax
from jax.experimental import pallas as pl
from jax.experimental.pallas import tpu as pltpu
from jax.sharding import Mesh, PartitionSpec as P

HD = 128
BLK = 128
VMEM_LIMIT = 48 * 1024 * 1024
DP = ("y", "z")


def from_behind(x, axis, by):
    count = lax.axis_size(axis)
    return lax.ppermute(x, axis, [(i, (i + by) % count) for i in range(count)])


def swap(x, axis):
    return lax.all_to_all(x, axis, split_axis=0, concat_axis=0, tiled=True)


def dot(a, b, dims):
    return lax.dot_general(a, b, (dims, ((), ())), preferred_element_type=jnp.float32)


def live_mask(ids_ref, cnt_ref, tokens, ctx):
    row = lax.broadcasted_iota(jnp.int32, (tokens, ctx), 0) // BLK
    col = lax.broadcasted_iota(jnp.int32, (tokens, ctx), 1) // BLK
    live = None
    for b in range(tokens // BLK):
        for k in range(ids_ref.shape[2]):
            block = jnp.where(k < cnt_ref[0, b], ids_ref[0, b, k], -1)
            here = (row == b) & (col == block)
            live = here if live is None else live | here
    return live


def forward_kernel(ids_ref, cnt_ref, q_ref, kv_ref, cot_ref, attn_ref, prob_ref, part_ref):
    tokens, width = q_ref.shape[1:]
    ctx = kv_ref.shape[2]
    live = live_mask(ids_ref, cnt_ref, tokens, ctx)
    scale = 1.0 / HD**0.5
    for h in range(width // HD):
        cols = slice(h * HD, (h + 1) * HD)
        score = dot(q_ref[0, :, cols], kv_ref[0, 0, :, cols], ((1,), (1,))) * scale
        score = jnp.where(live, score, jnp.float32(-1e30))
        expo = jnp.exp(score - jnp.max(score, axis=1, keepdims=True))
        prob = expo / jnp.sum(expo, axis=1, keepdims=True)
        prob_ref[h] = prob
        attn_ref[:, cols] = dot(
            prob.astype(jnp.bfloat16), kv_ref[0, 1, :, cols], ((1,), (0,))
        ).astype(jnp.bfloat16)
    first, second, rows, _ = part_ref.shape
    attn = attn_ref[...]
    for j in range(second):
        span = first * rows
        part = dot(cot_ref[0, :, j * span : (j + 1) * span], attn, ((0,), (0,)))
        for i in range(first):
            part_ref[i, j] = part[i * rows : (i + 1) * rows].astype(jnp.bfloat16)


def backward_kernel(q_ref, kv_ref, cot_ref, attn_ref, prob_ref, w_ref, gq_ref, gkv_ref):
    width = q_ref.shape[2]
    scale = 1.0 / HD**0.5
    d_attn = dot(cot_ref[0], w_ref[...], ((1,), (0,))).astype(jnp.bfloat16)
    for h in range(width // HD):
        cols = slice(h * HD, (h + 1) * HD)
        da = d_attn[:, cols]
        q, k, v = q_ref[0, :, cols], kv_ref[0, 0, :, cols], kv_ref[0, 1, :, cols]
        prob = prob_ref[h]
        delta = jnp.sum(
            da.astype(jnp.float32) * attn_ref[:, cols].astype(jnp.float32), axis=1, keepdims=True
        )
        dprob = dot(da, v, ((1,), (1,)))
        dscore = (prob * (dprob - delta)).astype(jnp.bfloat16)
        gq_ref[0, :, cols] = (dot(dscore, k, ((1,), (0,))) * scale).astype(jnp.bfloat16)
        gkv_ref[0, 0, :, cols] = (dot(dscore, q, ((0,), (0,))) * scale).astype(jnp.bfloat16)
        gkv_ref[0, 1, :, cols] = dot(prob.astype(jnp.bfloat16), da, ((0,), (0,))).astype(jnp.bfloat16)


def fold_kernel(parts_ref, total_ref):
    total = parts_ref[0].astype(jnp.float32)
    for i in range(1, parts_ref.shape[0]):
        total += parts_ref[i].astype(jnp.float32)
    total_ref[...] = total.astype(total_ref.dtype)


def fold(parts, dtype):
    vmem = pl.BlockSpec(memory_space=pltpu.VMEM)
    return pl.pallas_call(
        fold_kernel,
        name="fold",
        out_shape=jax.ShapeDtypeStruct(parts.shape[1:], dtype),
        in_specs=[vmem],
        out_specs=vmem,
        compiler_params=pltpu.CompilerParams(vmem_limit_bytes=VMEM_LIMIT),
        cost_estimate=pl.CostEstimate(flops=parts.size, bytes_accessed=2 * parts.size, transcendentals=0),
    )(parts)


def shards(queries, context, vis_blocks, vis_count, w_out, grad_out):
    tokens, width = queries.shape[1:]
    ctx = context.shape[2]
    heads = width // HD
    model = grad_out.shape[2]
    ny, nz = (lax.axis_size(a) for a in DP)
    rows = w_out.shape[1]
    smem = pl.BlockSpec(memory_space=pltpu.SMEM)
    vmem = pl.BlockSpec(memory_space=pltpu.VMEM)
    params = pltpu.CompilerParams(vmem_limit_bytes=VMEM_LIMIT)

    used = from_behind(context, "segment", 1)
    near = swap(jnp.broadcast_to(w_out, (nz, rows, width)), "z")
    weight = swap(jnp.broadcast_to(near[None], (ny, nz, rows, width)), "y").reshape(model, width)

    attn, prob, part = pl.pallas_call(
        forward_kernel,
        name="forward",
        out_shape=(
            jax.ShapeDtypeStruct((tokens, width), jnp.bfloat16),
            jax.ShapeDtypeStruct((heads, tokens, ctx), jnp.float32),
            jax.ShapeDtypeStruct((nz, ny, rows, width), jnp.bfloat16),
        ),
        in_specs=[smem, smem, vmem, vmem, vmem],
        out_specs=(vmem, vmem, vmem),
        compiler_params=params,
        cost_estimate=pl.CostEstimate(
            flops=2 * tokens * width * (2 * ctx + model), bytes_accessed=4 << 20, transcendentals=heads * tokens * ctx
        ),
    )(vis_blocks, vis_count, queries, used, grad_out)

    over_z = fold(swap(part, "z"), jnp.bfloat16)
    grad_weight = fold(swap(over_z, "y"), jnp.float32)[None]

    grad_q, grad_used = pl.pallas_call(
        backward_kernel,
        name="backward",
        out_shape=(
            jax.ShapeDtypeStruct(queries.shape, jnp.bfloat16),
            jax.ShapeDtypeStruct(context.shape, jnp.bfloat16),
        ),
        in_specs=[vmem] * 6,
        out_specs=(vmem, vmem),
        compiler_params=params,
        cost_estimate=pl.CostEstimate(
            flops=2 * tokens * width * (4 * ctx + model), bytes_accessed=4 << 20, transcendentals=0
        ),
    )(queries, used, grad_out, attn, prob, weight)
    grad_context = from_behind(grad_used, "segment", -1)
    return grad_q, grad_context, grad_weight


def solution(mesh):
    fine = Mesh(mesh.devices.reshape(4, 8, 8, 4), ("segment", "y", "z", "tensor"))
    in_specs = (
        P("segment", DP, "tensor"),
        P("segment", None, DP, "tensor"),
        P("segment", DP, None),
        P("segment", DP),
        P("segment", DP, "tensor"),
        P("segment", DP, None),
    )
    out_specs = (
        P("segment", DP, "tensor"),
        P("segment", None, DP, "tensor"),
        P("segment", DP, "tensor"),
    )
    return jax.shard_map(shards, mesh=fine, in_specs=in_specs, out_specs=out_specs, check_vma=False)
```

```python
import jax
import jax.numpy as jnp
from jax import lax
from jax.experimental import pallas as pl
from jax.experimental.pallas import tpu as pltpu
from jax.sharding import Mesh, PartitionSpec as P

HD = 128
BLK = 128
VMEM_LIMIT = 16 * 1024 * 1024
DP = ("y", "z")
PLANE = ("y", "z", "tensor")


def from_behind(x, axis, by):
    count = lax.axis_size(axis)
    return lax.ppermute(x, axis, [(i, (i + by) % count) for i in range(count)])


def lines(first):
    ny, nz, nt = (lax.axis_size(a) for a in PLANE)
    groups = []
    for t in range(nt):
        if (t % 2 == 0) == first:
            groups += [[(y * nz + z) * nt + t for z in range(nz)] for y in range(ny)]
        else:
            groups += [[(y * nz + z) * nt + t for y in range(ny)] for z in range(nz)]
    return groups


def swap(x, first):
    return lax.all_to_all(
        x, PLANE, split_axis=0, concat_axis=0, axis_index_groups=lines(first), tiled=True
    )


def dot(a, b, dims):
    return lax.dot_general(a, b, (dims, ((), ())), preferred_element_type=jnp.float32)


def live_mask(ids_ref, cnt_ref, tokens, ctx):
    row = lax.broadcasted_iota(jnp.int32, (tokens, ctx), 0) // BLK
    col = lax.broadcasted_iota(jnp.int32, (tokens, ctx), 1) // BLK
    live = None
    for b in range(tokens // BLK):
        for k in range(ids_ref.shape[2]):
            block = jnp.where(k < cnt_ref[0, b], ids_ref[0, b, k], -1)
            here = (row == b) & (col == block)
            live = here if live is None else live | here
    return live


def forward_kernel(ids_ref, cnt_ref, q_ref, kv_ref, cot_ref, attn_ref, prob_ref, part_ref):
    tokens, width = q_ref.shape[1:]
    ctx = kv_ref.shape[2]
    live = live_mask(ids_ref, cnt_ref, tokens, ctx)
    scale = 1.0 / HD**0.5
    for h in range(width // HD):
        cols = slice(h * HD, (h + 1) * HD)
        score = dot(q_ref[0, :, cols], kv_ref[0, 0, :, cols], ((1,), (1,))) * scale
        score = jnp.where(live, score, jnp.float32(-1e30))
        expo = jnp.exp(score - jnp.max(score, axis=1, keepdims=True))
        prob = expo / jnp.sum(expo, axis=1, keepdims=True)
        prob_ref[h] = prob
        attn_ref[:, cols] = dot(
            prob.astype(jnp.bfloat16), kv_ref[0, 1, :, cols], ((1,), (0,))
        ).astype(jnp.bfloat16)
    side, _, rows, _ = part_ref.shape
    attn = attn_ref[...]
    odd = lax.axis_index("tensor") % 2 == 1
    for y in range(side):
        span = side * rows
        part = dot(cot_ref[0, :, y * span : (y + 1) * span], attn, ((0,), (0,)))
        for z in range(side):
            block = part[z * rows : (z + 1) * rows].astype(jnp.bfloat16)
            part_ref[jnp.where(odd, y, z), jnp.where(odd, z, y)] = block


def backward_kernel(q_ref, kv_ref, cot_ref, attn_ref, prob_ref, w_ref, gq_ref, gkv_ref, rows_ref, sem):
    width = q_ref.shape[2]
    scale = 1.0 / HD**0.5
    side, _, rows, _ = w_ref.shape
    odd = lax.axis_index("tensor") % 2 == 1
    copies = [
        [
            pltpu.make_async_copy(
                w_ref.at[:, y] if turned else w_ref.at[y], rows_ref.at[y], sem.at[y]
            )
            for y in range(side)
        ]
        for turned in range(2)
    ]
    for turned in range(2):

        @pl.when(odd == (turned == 1))
        def _(turned=turned):
            for copy in copies[turned]:
                copy.start()

    d_attn = jnp.zeros((q_ref.shape[1], width), jnp.float32)
    span = side * rows
    for y in range(side):
        copies[0][y].wait()
        block = rows_ref[y].reshape(span, width)
        d_attn += dot(cot_ref[0, :, y * span : (y + 1) * span], block, ((1,), (0,)))
    d_attn = d_attn.astype(jnp.bfloat16)
    for h in range(width // HD):
        cols = slice(h * HD, (h + 1) * HD)
        da = d_attn[:, cols]
        q, k, v = q_ref[0, :, cols], kv_ref[0, 0, :, cols], kv_ref[0, 1, :, cols]
        prob = prob_ref[h]
        delta = jnp.sum(
            da.astype(jnp.float32) * attn_ref[:, cols].astype(jnp.float32), axis=1, keepdims=True
        )
        dprob = dot(da, v, ((1,), (1,)))
        dscore = (prob * (dprob - delta)).astype(jnp.bfloat16)
        gq_ref[0, :, cols] = (dot(dscore, k, ((1,), (0,))) * scale).astype(jnp.bfloat16)
        gkv_ref[0, 0, :, cols] = (dot(dscore, q, ((0,), (0,))) * scale).astype(jnp.bfloat16)
        gkv_ref[0, 1, :, cols] = dot(prob.astype(jnp.bfloat16), da, ((0,), (0,))).astype(jnp.bfloat16)


def fold_kernel(parts_ref, total_ref):
    total = parts_ref[0].astype(jnp.float32)
    for i in range(1, parts_ref.shape[0]):
        total += parts_ref[i].astype(jnp.float32)
    total_ref[...] = total.astype(total_ref.dtype)


def fold(parts, dtype):
    vmem = pl.BlockSpec(memory_space=pltpu.VMEM)
    return pl.pallas_call(
        fold_kernel,
        name="fold",
        out_shape=jax.ShapeDtypeStruct(parts.shape[1:], dtype),
        in_specs=[vmem],
        out_specs=vmem,
        compiler_params=pltpu.CompilerParams(vmem_limit_bytes=VMEM_LIMIT),
        cost_estimate=pl.CostEstimate(flops=parts.size, bytes_accessed=2 * parts.size, transcendentals=0),
    )(parts)


def shards(queries, context, vis_blocks, vis_count, w_out, grad_out):
    tokens, width = queries.shape[1:]
    ctx = context.shape[2]
    heads = width // HD
    model = grad_out.shape[2]
    ny, nz = (lax.axis_size(a) for a in DP)
    rows = w_out.shape[1]
    smem = pl.BlockSpec(memory_space=pltpu.SMEM)
    vmem = pl.BlockSpec(memory_space=pltpu.VMEM)
    params = pltpu.CompilerParams(vmem_limit_bytes=VMEM_LIMIT)

    used = from_behind(context, "segment", 1)
    near = swap(jnp.broadcast_to(w_out, (nz, rows, width)), True)
    weight = swap(jnp.broadcast_to(near[None], (ny, nz, rows, width)), False)

    attn, prob, part = pl.pallas_call(
        forward_kernel,
        name="forward",
        out_shape=(
            jax.ShapeDtypeStruct((tokens, width), jnp.bfloat16),
            jax.ShapeDtypeStruct((heads, tokens, ctx), jnp.float32),
            jax.ShapeDtypeStruct((nz, ny, rows, width), jnp.bfloat16),
        ),
        in_specs=[smem, smem, vmem, vmem, vmem],
        out_specs=(vmem, vmem, vmem),
        compiler_params=params,
        cost_estimate=pl.CostEstimate(
            flops=2 * tokens * width * (2 * ctx + model), bytes_accessed=4 << 20, transcendentals=heads * tokens * ctx
        ),
    )(vis_blocks, vis_count, queries, used, grad_out)

    once = fold(swap(part, True), jnp.bfloat16)
    grad_weight = fold(swap(once, False), jnp.float32)[None]

    grad_q, grad_used = pl.pallas_call(
        backward_kernel,
        name="backward",
        out_shape=(
            jax.ShapeDtypeStruct(queries.shape, jnp.bfloat16),
            jax.ShapeDtypeStruct(context.shape, jnp.bfloat16),
        ),
        in_specs=[vmem] * 5 + [pl.BlockSpec(memory_space=pl.ANY)],
        out_specs=(vmem, vmem),
        scratch_shapes=[
            pltpu.VMEM((ny, nz, rows, width), jnp.bfloat16),
            pltpu.SemaphoreType.DMA((ny,)),
        ],
        compiler_params=params,
        cost_estimate=pl.CostEstimate(
            flops=2 * tokens * width * (4 * ctx + model), bytes_accessed=4 << 20, transcendentals=0
        ),
    )(queries, used, grad_out, attn, prob, weight)
    grad_context = from_behind(grad_used, "segment", -1)
    return grad_q, grad_context, grad_weight


def solution(mesh):
    fine = Mesh(mesh.devices.reshape(4, 8, 8, 4), ("segment", "y", "z", "tensor"))
    in_specs = (
        P("segment", DP, "tensor"),
        P("segment", None, DP, "tensor"),
        P("segment", DP, None),
        P("segment", DP),
        P("segment", DP, "tensor"),
        P("segment", DP, None),
    )
    out_specs = (
        P("segment", DP, "tensor"),
        P("segment", None, DP, "tensor"),
        P("segment", DP, "tensor"),
    )
    return jax.shard_map(shards, mesh=fine, in_specs=in_specs, out_specs=out_specs, check_vma=False)
```

```python
import jax
import jax.numpy as jnp
from jax import lax
from jax.experimental import pallas as pl
from jax.experimental.pallas import tpu as pltpu
from jax.sharding import Mesh, PartitionSpec as P

HD = 128
BLK = 128
VMEM_LIMIT = 16 * 1024 * 1024
DP = ("y", "z")
PLANE = ("y", "z", "tensor")


def from_behind(x, axis, by):
    count = lax.axis_size(axis)
    return lax.ppermute(x, axis, [(i, (i + by) % count) for i in range(count)])


def lines(first):
    ny, nz, nt = (lax.axis_size(a) for a in PLANE)
    groups = []
    for t in range(nt):
        if (t % 2 == 0) == first:
            groups += [[(y * nz + z) * nt + t for z in range(nz)] for y in range(ny)]
        else:
            groups += [[(y * nz + z) * nt + t for y in range(ny)] for z in range(nz)]
    return groups


def swap(x, first):
    return lax.all_to_all(
        x, PLANE, split_axis=0, concat_axis=0, axis_index_groups=lines(first), tiled=True
    )


def dot(a, b, dims):
    return lax.dot_general(a, b, (dims, ((), ())), preferred_element_type=jnp.float32)


def live_mask(ids_ref, cnt_ref, tokens, ctx):
    row = lax.broadcasted_iota(jnp.int32, (tokens, ctx), 0) // BLK
    col = lax.broadcasted_iota(jnp.int32, (tokens, ctx), 1) // BLK
    live = None
    for b in range(tokens // BLK):
        for k in range(ids_ref.shape[2]):
            block = jnp.where(k < cnt_ref[0, b], ids_ref[0, b, k], -1)
            here = (row == b) & (col == block)
            live = here if live is None else live | here
    return live


def forward_kernel(ids_ref, cnt_ref, q_ref, kv_ref, cot_ref, attn_ref, prob_ref, part_ref):
    tokens, width = q_ref.shape[1:]
    ctx = kv_ref.shape[2]
    live = live_mask(ids_ref, cnt_ref, tokens, ctx)
    scale = 1.0 / HD**0.5
    for h in range(width // HD):
        cols = slice(h * HD, (h + 1) * HD)
        score = dot(q_ref[0, :, cols], kv_ref[0, 0, :, cols], ((1,), (1,))) * scale
        score = jnp.where(live, score, jnp.float32(-1e30))
        expo = jnp.exp(score - jnp.max(score, axis=1, keepdims=True))
        prob = expo / jnp.sum(expo, axis=1, keepdims=True)
        prob_ref[h] = prob
        attn_ref[:, cols] = dot(
            prob.astype(jnp.bfloat16), kv_ref[0, 1, :, cols], ((1,), (0,))
        ).astype(jnp.bfloat16)
    side, _, rows, _ = part_ref.shape
    attn = attn_ref[...]
    odd = lax.axis_index("tensor") % 2 == 1
    for y in range(side):
        span = side * rows
        part = dot(cot_ref[0, :, y * span : (y + 1) * span], attn, ((0,), (0,)))
        for z in range(side):
            block = part[z * rows : (z + 1) * rows].astype(jnp.bfloat16)
            part_ref[jnp.where(odd, y, z), jnp.where(odd, z, y)] = block


def backward_kernel(q_ref, kv_ref, cot_ref, attn_ref, prob_ref, w_ref, gq_ref, gkv_ref, rows_ref, sem):
    width = q_ref.shape[2]
    scale = 1.0 / HD**0.5
    side, _, rows, _ = w_ref.shape
    odd = lax.axis_index("tensor") % 2 == 1
    copies = [
        [
            pltpu.make_async_copy(
                w_ref.at[:, y] if turned else w_ref.at[y], rows_ref.at[y], sem.at[y]
            )
            for y in range(side)
        ]
        for turned in range(2)
    ]
    for turned in range(2):

        @pl.when(odd == (turned == 1))
        def _(turned=turned):
            for copy in copies[turned]:
                copy.start()

    d_attn = jnp.zeros((q_ref.shape[1], width), jnp.float32)
    span = side * rows
    for y in range(side):
        copies[0][y].wait()
        block = rows_ref[y].reshape(span, width)
        d_attn += dot(cot_ref[0, :, y * span : (y + 1) * span], block, ((1,), (0,)))
    d_attn = d_attn.astype(jnp.bfloat16)
    for h in range(width // HD):
        cols = slice(h * HD, (h + 1) * HD)
        da = d_attn[:, cols]
        q, k, v = q_ref[0, :, cols], kv_ref[0, 0, :, cols], kv_ref[0, 1, :, cols]
        prob = prob_ref[h]
        delta = jnp.sum(
            da.astype(jnp.float32) * attn_ref[:, cols].astype(jnp.float32), axis=1, keepdims=True
        )
        dprob = dot(da, v, ((1,), (1,)))
        dscore = (prob * (dprob - delta)).astype(jnp.bfloat16)
        gq_ref[0, :, cols] = (dot(dscore, k, ((1,), (0,))) * scale).astype(jnp.bfloat16)
        gkv_ref[0, 0, :, cols] = (dot(dscore, q, ((0,), (0,))) * scale).astype(jnp.bfloat16)
        gkv_ref[0, 1, :, cols] = dot(prob.astype(jnp.bfloat16), da, ((0,), (0,))).astype(jnp.bfloat16)


def fold_kernel(parts_ref, total_ref):
    total = parts_ref[0].astype(jnp.float32)
    for i in range(1, parts_ref.shape[0]):
        total += parts_ref[i].astype(jnp.float32)
    total_ref[...] = total.astype(total_ref.dtype)


def fold(parts, dtype):
    vmem = pl.BlockSpec(memory_space=pltpu.VMEM)
    return pl.pallas_call(
        fold_kernel,
        name="fold",
        out_shape=jax.ShapeDtypeStruct(parts.shape[1:], dtype),
        in_specs=[vmem],
        out_specs=vmem,
        compiler_params=pltpu.CompilerParams(vmem_limit_bytes=VMEM_LIMIT),
        cost_estimate=pl.CostEstimate(flops=parts.size, bytes_accessed=2 * parts.size, transcendentals=0),
    )(parts)


def shards(queries, context, vis_blocks, vis_count, w_out, grad_out):
    tokens, width = queries.shape[1:]
    ctx = context.shape[2]
    heads = width // HD
    model = grad_out.shape[2]
    ny, nz = (lax.axis_size(a) for a in DP)
    rows = w_out.shape[1]
    smem = pl.BlockSpec(memory_space=pltpu.SMEM)
    vmem = pl.BlockSpec(memory_space=pltpu.VMEM)
    params = pltpu.CompilerParams(vmem_limit_bytes=VMEM_LIMIT)

    used = from_behind(context, "segment", 1)
    near = swap(jnp.broadcast_to(w_out, (nz, rows, width)), True)
    weight = lax.all_gather(near, PLANE, axis=0, axis_index_groups=lines(False))

    attn, prob, part = pl.pallas_call(
        forward_kernel,
        name="forward",
        out_shape=(
            jax.ShapeDtypeStruct((tokens, width), jnp.bfloat16),
            jax.ShapeDtypeStruct((heads, tokens, ctx), jnp.float32),
            jax.ShapeDtypeStruct((nz, ny, rows, width), jnp.bfloat16),
        ),
        in_specs=[smem, smem, vmem, vmem, vmem],
        out_specs=(vmem, vmem, vmem),
        compiler_params=params,
        cost_estimate=pl.CostEstimate(
            flops=2 * tokens * width * (2 * ctx + model), bytes_accessed=4 << 20, transcendentals=heads * tokens * ctx
        ),
    )(vis_blocks, vis_count, queries, used, grad_out)

    once = fold(swap(part, True), jnp.bfloat16)
    grad_weight = fold(swap(once, False), jnp.float32)[None]

    grad_q, grad_used = pl.pallas_call(
        backward_kernel,
        name="backward",
        out_shape=(
            jax.ShapeDtypeStruct(queries.shape, jnp.bfloat16),
            jax.ShapeDtypeStruct(context.shape, jnp.bfloat16),
        ),
        in_specs=[vmem] * 5 + [pl.BlockSpec(memory_space=pl.ANY)],
        out_specs=(vmem, vmem),
        scratch_shapes=[
            pltpu.VMEM((ny, nz, rows, width), jnp.bfloat16),
            pltpu.SemaphoreType.DMA((ny,)),
        ],
        compiler_params=params,
        cost_estimate=pl.CostEstimate(
            flops=2 * tokens * width * (4 * ctx + model), bytes_accessed=4 << 20, transcendentals=0
        ),
    )(queries, used, grad_out, attn, prob, weight)
    grad_context = from_behind(grad_used, "segment", -1)
    return grad_q, grad_context, grad_weight


def solution(mesh):
    fine = Mesh(mesh.devices.reshape(4, 8, 8, 4), ("segment", "y", "z", "tensor"))
    in_specs = (
        P("segment", DP, "tensor"),
        P("segment", None, DP, "tensor"),
        P("segment", DP, None),
        P("segment", DP),
        P("segment", DP, "tensor"),
        P("segment", DP, None),
    )
    out_specs = (
        P("segment", DP, "tensor"),
        P("segment", None, DP, "tensor"),
        P("segment", DP, "tensor"),
    )
    return jax.shard_map(shards, mesh=fine, in_specs=in_specs, out_specs=out_specs, check_vma=False)
```

```python
import jax
import jax.numpy as jnp
from jax import lax
from jax.experimental import pallas as pl
from jax.experimental.pallas import tpu as pltpu
from jax.sharding import Mesh, PartitionSpec as P

HD = 128
BLK = 128
VMEM_LIMIT = 16 * 1024 * 1024
SCALE = 1.0 / HD**0.5
DP = ("y", "z")
PLANE = ("y", "z", "tensor")


def from_behind(x, axis, by):
    count = lax.axis_size(axis)
    return lax.ppermute(x, axis, [(i, (i + by) % count) for i in range(count)])


def lines(first):
    ny, nz, nt = (lax.axis_size(a) for a in PLANE)
    groups = []
    for t in range(nt):
        if (t % 2 == 0) == first:
            groups += [[(y * nz + z) * nt + t for z in range(nz)] for y in range(ny)]
        else:
            groups += [[(y * nz + z) * nt + t for y in range(ny)] for z in range(nz)]
    return groups


def swap(x, first):
    return lax.all_to_all(
        x, PLANE, split_axis=0, concat_axis=0, axis_index_groups=lines(first), tiled=True
    )


def mirror(x, distance):
    pairs = [(line[i], line[i ^ distance]) for line in lines(False) for i in range(len(line))]
    return lax.ppermute(x, PLANE, pairs)


def gather_slots(near):
    pieces = [(near[None], [0])]
    distance = len(lines(False)[0]) // 2
    while distance:
        if len(pieces) == 2 and distance > 1:
            pieces = [(jnp.concatenate([a for a, _ in pieces]), [s for _, k in pieces for s in k])]
        pieces += [(mirror(a, distance), [s ^ distance for s in k]) for a, k in pieces]
        distance //= 2
    return pieces


def dot(a, b, dims):
    return lax.dot_general(a, b, (dims, ((), ())), preferred_element_type=jnp.float32)


def live_mask(ids_ref, cnt_ref, tokens, ctx):
    row = lax.broadcasted_iota(jnp.int32, (tokens, ctx), 0) // BLK
    col = lax.broadcasted_iota(jnp.int32, (tokens, ctx), 1) // BLK
    live = None
    for b in range(tokens // BLK):
        for k in range(ids_ref.shape[2]):
            block = jnp.where(k < cnt_ref[0, b], ids_ref[0, b, k], -1)
            here = (row == b) & (col == block)
            live = here if live is None else live | here
    return live


def softmax(q, k, live):
    score = jnp.where(live, dot(q, k, ((1,), (1,))) * SCALE, jnp.float32(-1e30))
    expo = jnp.exp(score - jnp.max(score, axis=1, keepdims=True))
    return expo / jnp.sum(expo, axis=1, keepdims=True)


def forward_kernel(
    ids_hbm, cnt_hbm, q_hbm, kv_hbm, cot_hbm, part_ref, ids_ref, cnt_ref, q_ref, kv_ref, cot_ref, attn_ref, sem
):
    copies = [
        pltpu.make_async_copy(src, dst, sem.at[i])
        for i, (src, dst) in enumerate(
            [(ids_hbm, ids_ref), (cnt_hbm, cnt_ref), (q_hbm, q_ref), (kv_hbm, kv_ref), (cot_hbm, cot_ref)]
        )
    ]
    for copy in copies:
        copy.start()
    tokens, width = q_ref.shape[1:]
    for copy in copies[:4]:
        copy.wait()
    live = live_mask(ids_ref, cnt_ref, tokens, kv_ref.shape[2])
    for h in range(width // HD):
        cols = slice(h * HD, (h + 1) * HD)
        prob = softmax(q_ref[0, :, cols], kv_ref[0, 0, :, cols], live).astype(jnp.bfloat16)
        attn_ref[:, cols] = dot(prob, kv_ref[0, 1, :, cols], ((1,), (0,))).astype(jnp.bfloat16)
    copies[4].wait()
    side, _, rows, _ = part_ref.shape
    attn = attn_ref[...]
    odd = lax.axis_index("tensor") % 2 == 1
    for y in range(side):
        span = side * rows
        part = dot(cot_ref[0, :, y * span : (y + 1) * span], attn, ((0,), (0,)))
        for z in range(side):
            block = part[z * rows : (z + 1) * rows].astype(jnp.bfloat16)
            part_ref[jnp.where(odd, y, z), jnp.where(odd, z, y)] = block


def backward_kernel(slots, ids_hbm, cnt_hbm, q_hbm, kv_hbm, cot_hbm, *refs):
    pieces = refs[: len(slots)]
    gq_ref, gkv_ref, ids_ref, cnt_ref, q_ref, kv_ref, cot_ref, rows_ref, sem, slot_sem = refs[len(slots) :]
    copies = [
        pltpu.make_async_copy(src, dst, sem.at[i])
        for i, (src, dst) in enumerate(
            [(ids_hbm, ids_ref), (cnt_hbm, cnt_ref), (q_hbm, q_ref), (kv_hbm, kv_ref), (cot_hbm, cot_ref)]
        )
    ]
    for copy in copies:
        copy.start()
    odd = lax.axis_index("tensor") % 2 == 1
    placed = []
    for turned in range(2):
        place = lax.axis_index(DP[1] if turned else DP[0])
        moves = []
        for piece, held in zip(pieces, slots):
            for i, k in enumerate(held):
                at = place ^ k
                target = rows_ref.at[:, at] if turned else rows_ref.at[at]
                moves.append(pltpu.make_async_copy(piece.at[i], target, slot_sem.at[k]))
        placed.append(moves)

        @pl.when(odd == (turned == 1))
        def _(moves=moves):
            for move in moves:
                move.start()

    tokens, width = q_ref.shape[1:]
    for copy in copies[:4]:
        copy.wait()
    live = live_mask(ids_ref, cnt_ref, tokens, kv_ref.shape[2])
    side, _, rows, _ = rows_ref.shape
    probs = []
    attns = []
    for h in range(width // HD):
        cols = slice(h * HD, (h + 1) * HD)
        prob = softmax(q_ref[0, :, cols], kv_ref[0, 0, :, cols], live)
        probs.append(prob)
        attns.append(
            dot(prob.astype(jnp.bfloat16), kv_ref[0, 1, :, cols], ((1,), (0,))).astype(jnp.bfloat16)
        )
    copies[4].wait()
    for move in placed[0]:
        move.wait()
    weight = rows_ref[...].reshape(side * side * rows, width)
    d_attn = dot(cot_ref[0], weight, ((1,), (0,))).astype(jnp.bfloat16)
    for h in range(width // HD):
        cols = slice(h * HD, (h + 1) * HD)
        da = d_attn[:, cols]
        q, k, v = q_ref[0, :, cols], kv_ref[0, 0, :, cols], kv_ref[0, 1, :, cols]
        prob = probs[h]
        delta = jnp.sum(da.astype(jnp.float32) * attns[h].astype(jnp.float32), axis=1, keepdims=True)
        dprob = dot(da, v, ((1,), (1,)))
        dscore = (prob * (dprob - delta)).astype(jnp.bfloat16)
        gq_ref[0, :, cols] = (dot(dscore, k, ((1,), (0,))) * SCALE).astype(jnp.bfloat16)
        gkv_ref[0, 0, :, cols] = (dot(dscore, q, ((0,), (0,))) * SCALE).astype(jnp.bfloat16)
        gkv_ref[0, 1, :, cols] = dot(prob.astype(jnp.bfloat16), da, ((0,), (0,))).astype(jnp.bfloat16)


def fold_kernel(parts_ref, total_ref):
    total = parts_ref[0].astype(jnp.float32)
    for i in range(1, parts_ref.shape[0]):
        total += parts_ref[i].astype(jnp.float32)
    total_ref[...] = total.astype(total_ref.dtype)


def fold(parts, dtype):
    vmem = pl.BlockSpec(memory_space=pltpu.VMEM)
    return pl.pallas_call(
        fold_kernel,
        name="fold",
        out_shape=jax.ShapeDtypeStruct(parts.shape[1:], dtype),
        in_specs=[vmem],
        out_specs=vmem,
        compiler_params=pltpu.CompilerParams(vmem_limit_bytes=VMEM_LIMIT),
        cost_estimate=pl.CostEstimate(flops=parts.size, bytes_accessed=2 * parts.size, transcendentals=0),
    )(parts)


def shards(queries, context, vis_blocks, vis_count, w_out, grad_out):
    tokens, width = queries.shape[1:]
    ctx = context.shape[2]
    heads = width // HD
    model = grad_out.shape[2]
    ny, nz = (lax.axis_size(a) for a in DP)
    rows = w_out.shape[1]
    hbm = pl.BlockSpec(memory_space=pltpu.HBM)
    anywhere = pl.BlockSpec(memory_space=pl.ANY)
    vmem = pl.BlockSpec(memory_space=pltpu.VMEM)
    params = pltpu.CompilerParams(vmem_limit_bytes=VMEM_LIMIT)
    small = [
        pltpu.SMEM(vis_blocks.shape, jnp.int32),
        pltpu.SMEM(vis_count.shape, jnp.int32),
        pltpu.VMEM(queries.shape, jnp.bfloat16),
        pltpu.VMEM(context.shape, jnp.bfloat16),
        pltpu.VMEM(grad_out.shape, jnp.bfloat16),
    ]

    used = from_behind(context, "segment", 1)
    near = swap(jnp.broadcast_to(w_out, (nz, rows, width)), True)
    used, near = lax.optimization_barrier((used, near))
    fixed = [pltpu.with_memory_space_constraint(a, pltpu.HBM) for a in (vis_blocks, vis_count, queries)]
    cotan = pltpu.with_memory_space_constraint(grad_out, pltpu.HBM)

    part = pl.pallas_call(
        forward_kernel,
        name="forward",
        out_shape=jax.ShapeDtypeStruct((nz, ny, rows, width), jnp.bfloat16),
        in_specs=[hbm, hbm, hbm, anywhere, hbm],
        out_specs=vmem,
        scratch_shapes=small + [pltpu.VMEM((tokens, width), jnp.bfloat16), pltpu.SemaphoreType.DMA((5,))],
        compiler_params=params,
        cost_estimate=pl.CostEstimate(
            flops=2 * tokens * width * (2 * ctx + model), bytes_accessed=3 << 20, transcendentals=heads * tokens * ctx
        ),
    )(*fixed, used, cotan)

    once = fold(swap(part, True), jnp.bfloat16)
    grad_weight = fold(swap(once, False), jnp.float32)[None]

    pieces = gather_slots(near)
    slots = [k for _, k in pieces]
    grad_q, grad_used = pl.pallas_call(
        lambda *refs: backward_kernel(slots, *refs),
        name="backward",
        out_shape=(
            jax.ShapeDtypeStruct(queries.shape, jnp.bfloat16),
            jax.ShapeDtypeStruct(context.shape, jnp.bfloat16),
        ),
        in_specs=[hbm, hbm, hbm, anywhere, hbm] + [anywhere] * len(pieces),
        out_specs=(vmem, vmem),
        scratch_shapes=small
        + [
            pltpu.VMEM((ny, nz, rows, width), jnp.bfloat16),
            pltpu.SemaphoreType.DMA((5,)),
            pltpu.SemaphoreType.DMA((ny,)),
        ],
        compiler_params=params,
        cost_estimate=pl.CostEstimate(
            flops=2 * tokens * width * (6 * ctx + model), bytes_accessed=4 << 20, transcendentals=heads * tokens * ctx
        ),
    )(*fixed, used, cotan, *(a for a, _ in pieces))
    grad_context = from_behind(grad_used, "segment", -1)
    return grad_q, grad_context, grad_weight


def solution(mesh):
    fine = Mesh(mesh.devices.reshape(4, 8, 8, 4), ("segment", "y", "z", "tensor"))
    in_specs = (
        P("segment", DP, "tensor"),
        P("segment", None, DP, "tensor"),
        P("segment", DP, None),
        P("segment", DP),
        P("segment", DP, "tensor"),
        P("segment", DP, None),
    )
    out_specs = (
        P("segment", DP, "tensor"),
        P("segment", None, DP, "tensor"),
        P("segment", DP, "tensor"),
    )
    return jax.shard_map(shards, mesh=fine, in_specs=in_specs, out_specs=out_specs, check_vma=False)
```

```python
import jax
import jax.numpy as jnp
from jax import lax
from jax.experimental import pallas as pl
from jax.experimental.pallas import tpu as pltpu
from jax.sharding import Mesh, PartitionSpec as P

HD = 128
BLK = 128
VMEM_LIMIT = 16 * 1024 * 1024
SCALE = 1.0 / HD**0.5
DP = ("y", "z")
PLANE = ("y", "z", "tensor")


def from_behind(x, axis, by):
    count = lax.axis_size(axis)
    return lax.ppermute(x, axis, [(i, (i + by) % count) for i in range(count)])


def lines(first):
    ny, nz, nt = (lax.axis_size(a) for a in PLANE)
    groups = []
    for t in range(nt):
        if (t % 2 == 0) == first:
            groups += [[(y * nz + z) * nt + t for z in range(nz)] for y in range(ny)]
        else:
            groups += [[(y * nz + z) * nt + t for y in range(ny)] for z in range(nz)]
    return groups


def swap(x, first):
    return lax.all_to_all(
        x, PLANE, split_axis=0, concat_axis=0, axis_index_groups=lines(first), tiled=True
    )


def mirror(x, distance):
    pairs = [(line[i], line[i ^ distance]) for line in lines(False) for i in range(len(line))]
    return lax.ppermute(x, PLANE, pairs)


def gather_slots(near):
    own = near[None]
    return [(own, [0])] + [(mirror(own, k), [k]) for k in range(1, len(lines(False)[0]))]


def dot(a, b, dims):
    return lax.dot_general(a, b, (dims, ((), ())), preferred_element_type=jnp.float32)


def live_mask(ids_ref, cnt_ref, tokens, ctx):
    row = lax.broadcasted_iota(jnp.int32, (tokens, ctx), 0) // BLK
    col = lax.broadcasted_iota(jnp.int32, (tokens, ctx), 1) // BLK
    live = None
    for b in range(tokens // BLK):
        for k in range(ids_ref.shape[2]):
            block = jnp.where(k < cnt_ref[0, b], ids_ref[0, b, k], -1)
            here = (row == b) & (col == block)
            live = here if live is None else live | here
    return live


def softmax(q, k, live):
    score = jnp.where(live, dot(q, k, ((1,), (1,))) * SCALE, jnp.float32(-1e30))
    expo = jnp.exp(score - jnp.max(score, axis=1, keepdims=True))
    return expo / jnp.sum(expo, axis=1, keepdims=True)


def forward_kernel(
    ids_hbm, cnt_hbm, q_hbm, kv_hbm, cot_hbm, part_ref, ids_ref, cnt_ref, q_ref, kv_ref, cot_ref, attn_ref, sem
):
    copies = [
        pltpu.make_async_copy(src, dst, sem.at[i])
        for i, (src, dst) in enumerate(
            [(ids_hbm, ids_ref), (cnt_hbm, cnt_ref), (q_hbm, q_ref), (kv_hbm, kv_ref), (cot_hbm, cot_ref)]
        )
    ]
    for copy in copies:
        copy.start()
    tokens, width = q_ref.shape[1:]
    for copy in copies[:4]:
        copy.wait()
    live = live_mask(ids_ref, cnt_ref, tokens, kv_ref.shape[2])
    for h in range(width // HD):
        cols = slice(h * HD, (h + 1) * HD)
        prob = softmax(q_ref[0, :, cols], kv_ref[0, 0, :, cols], live).astype(jnp.bfloat16)
        attn_ref[:, cols] = dot(prob, kv_ref[0, 1, :, cols], ((1,), (0,))).astype(jnp.bfloat16)
    copies[4].wait()
    side, _, rows, _ = part_ref.shape
    attn = attn_ref[...]
    odd = lax.axis_index("tensor") % 2 == 1
    for y in range(side):
        span = side * rows
        part = dot(cot_ref[0, :, y * span : (y + 1) * span], attn, ((0,), (0,)))
        for z in range(side):
            block = part[z * rows : (z + 1) * rows].astype(jnp.bfloat16)
            part_ref[jnp.where(odd, y, z), jnp.where(odd, z, y)] = block


def backward_kernel(slots, ids_hbm, cnt_hbm, q_hbm, kv_hbm, cot_hbm, *refs):
    pieces = refs[: len(slots)]
    gq_ref, gkv_ref, ids_ref, cnt_ref, q_ref, kv_ref, cot_ref, rows_ref, sem, slot_sem = refs[len(slots) :]
    copies = [
        pltpu.make_async_copy(src, dst, sem.at[i])
        for i, (src, dst) in enumerate(
            [(ids_hbm, ids_ref), (cnt_hbm, cnt_ref), (q_hbm, q_ref), (kv_hbm, kv_ref), (cot_hbm, cot_ref)]
        )
    ]
    for copy in copies:
        copy.start()
    odd = lax.axis_index("tensor") % 2 == 1
    placed = []
    for turned in range(2):
        place = lax.axis_index(DP[1] if turned else DP[0])
        moves = []
        for piece, held in zip(pieces, slots):
            for i, k in enumerate(held):
                at = place ^ k
                target = rows_ref.at[:, at] if turned else rows_ref.at[at]
                moves.append(pltpu.make_async_copy(piece.at[i], target, slot_sem.at[k]))
        placed.append(moves)

        @pl.when(odd == (turned == 1))
        def _(moves=moves):
            for move in moves:
                move.start()

    tokens, width = q_ref.shape[1:]
    for copy in copies[:4]:
        copy.wait()
    live = live_mask(ids_ref, cnt_ref, tokens, kv_ref.shape[2])
    side, _, rows, _ = rows_ref.shape
    probs = []
    attns = []
    for h in range(width // HD):
        cols = slice(h * HD, (h + 1) * HD)
        prob = softmax(q_ref[0, :, cols], kv_ref[0, 0, :, cols], live)
        probs.append(prob)
        attns.append(
            dot(prob.astype(jnp.bfloat16), kv_ref[0, 1, :, cols], ((1,), (0,))).astype(jnp.bfloat16)
        )
    copies[4].wait()
    for move in placed[0]:
        move.wait()
    weight = rows_ref[...].reshape(side * side * rows, width)
    d_attn = dot(cot_ref[0], weight, ((1,), (0,))).astype(jnp.bfloat16)
    for h in range(width // HD):
        cols = slice(h * HD, (h + 1) * HD)
        da = d_attn[:, cols]
        q, k, v = q_ref[0, :, cols], kv_ref[0, 0, :, cols], kv_ref[0, 1, :, cols]
        prob = probs[h]
        delta = jnp.sum(da.astype(jnp.float32) * attns[h].astype(jnp.float32), axis=1, keepdims=True)
        dprob = dot(da, v, ((1,), (1,)))
        dscore = (prob * (dprob - delta)).astype(jnp.bfloat16)
        gq_ref[0, :, cols] = (dot(dscore, k, ((1,), (0,))) * SCALE).astype(jnp.bfloat16)
        gkv_ref[0, 0, :, cols] = (dot(dscore, q, ((0,), (0,))) * SCALE).astype(jnp.bfloat16)
        gkv_ref[0, 1, :, cols] = dot(prob.astype(jnp.bfloat16), da, ((0,), (0,))).astype(jnp.bfloat16)


def fold_kernel(parts_ref, total_ref):
    total = parts_ref[0].astype(jnp.float32)
    for i in range(1, parts_ref.shape[0]):
        total += parts_ref[i].astype(jnp.float32)
    total_ref[...] = total.astype(total_ref.dtype)


def fold(parts, dtype):
    vmem = pl.BlockSpec(memory_space=pltpu.VMEM)
    return pl.pallas_call(
        fold_kernel,
        name="fold",
        out_shape=jax.ShapeDtypeStruct(parts.shape[1:], dtype),
        in_specs=[vmem],
        out_specs=vmem,
        compiler_params=pltpu.CompilerParams(vmem_limit_bytes=VMEM_LIMIT),
        cost_estimate=pl.CostEstimate(flops=parts.size, bytes_accessed=2 * parts.size, transcendentals=0),
    )(parts)


def shards(queries, context, vis_blocks, vis_count, w_out, grad_out):
    tokens, width = queries.shape[1:]
    ctx = context.shape[2]
    heads = width // HD
    model = grad_out.shape[2]
    ny, nz = (lax.axis_size(a) for a in DP)
    rows = w_out.shape[1]
    hbm = pl.BlockSpec(memory_space=pltpu.HBM)
    anywhere = pl.BlockSpec(memory_space=pl.ANY)
    vmem = pl.BlockSpec(memory_space=pltpu.VMEM)
    params = pltpu.CompilerParams(vmem_limit_bytes=VMEM_LIMIT)
    small = [
        pltpu.SMEM(vis_blocks.shape, jnp.int32),
        pltpu.SMEM(vis_count.shape, jnp.int32),
        pltpu.VMEM(queries.shape, jnp.bfloat16),
        pltpu.VMEM(context.shape, jnp.bfloat16),
        pltpu.VMEM(grad_out.shape, jnp.bfloat16),
    ]

    used = from_behind(context, "segment", 1)
    near = swap(jnp.broadcast_to(w_out, (nz, rows, width)), True)
    fixed = [pltpu.with_memory_space_constraint(a, pltpu.HBM) for a in (vis_blocks, vis_count, queries)]
    cotan = pltpu.with_memory_space_constraint(grad_out, pltpu.HBM)

    part = pl.pallas_call(
        forward_kernel,
        name="forward",
        out_shape=jax.ShapeDtypeStruct((nz, ny, rows, width), jnp.bfloat16),
        in_specs=[hbm, hbm, hbm, anywhere, hbm],
        out_specs=vmem,
        scratch_shapes=small + [pltpu.VMEM((tokens, width), jnp.bfloat16), pltpu.SemaphoreType.DMA((5,))],
        compiler_params=params,
        cost_estimate=pl.CostEstimate(
            flops=2 * tokens * width * (2 * ctx + model), bytes_accessed=3 << 20, transcendentals=heads * tokens * ctx
        ),
    )(*fixed, used, cotan)

    once = fold(swap(part, True), jnp.bfloat16)
    grad_weight = fold(swap(once, False), jnp.float32)[None]

    pieces = gather_slots(near)
    slots = [k for _, k in pieces]
    grad_q, grad_used = pl.pallas_call(
        lambda *refs: backward_kernel(slots, *refs),
        name="backward",
        out_shape=(
            jax.ShapeDtypeStruct(queries.shape, jnp.bfloat16),
            jax.ShapeDtypeStruct(context.shape, jnp.bfloat16),
        ),
        in_specs=[hbm, hbm, hbm, anywhere, hbm] + [anywhere] * len(pieces),
        out_specs=(vmem, vmem),
        scratch_shapes=small
        + [
            pltpu.VMEM((ny, nz, rows, width), jnp.bfloat16),
            pltpu.SemaphoreType.DMA((5,)),
            pltpu.SemaphoreType.DMA((ny,)),
        ],
        compiler_params=params,
        cost_estimate=pl.CostEstimate(
            flops=2 * tokens * width * (6 * ctx + model), bytes_accessed=4 << 20, transcendentals=heads * tokens * ctx
        ),
    )(*fixed, used, cotan, *(a for a, _ in pieces))
    grad_context = from_behind(grad_used, "segment", -1)
    return grad_q, grad_context, grad_weight


def solution(mesh):
    fine = Mesh(mesh.devices.reshape(4, 8, 8, 4), ("segment", "y", "z", "tensor"))
    in_specs = (
        P("segment", DP, "tensor"),
        P("segment", None, DP, "tensor"),
        P("segment", DP, None),
        P("segment", DP),
        P("segment", DP, "tensor"),
        P("segment", DP, None),
    )
    out_specs = (
        P("segment", DP, "tensor"),
        P("segment", None, DP, "tensor"),
        P("segment", DP, "tensor"),
    )
    return jax.shard_map(shards, mesh=fine, in_specs=in_specs, out_specs=out_specs, check_vma=False)
```

```python
import jax
import jax.numpy as jnp
from jax import lax
from jax.experimental import pallas as pl
from jax.experimental.pallas import tpu as pltpu
from jax.sharding import Mesh, PartitionSpec as P

HD = 128
BLK = 128
VMEM_LIMIT = 16 * 1024 * 1024
SCALE = 1.0 / HD**0.5
DP = ("y", "z")
PLANE = ("y", "z", "tensor")


def from_behind(x, axis, by):
    count = lax.axis_size(axis)
    return lax.ppermute(x, axis, [(i, (i + by) % count) for i in range(count)])


def lines(first):
    ny, nz, nt = (lax.axis_size(a) for a in PLANE)
    groups = []
    for t in range(nt):
        if (t % 2 == 0) == first:
            groups += [[(y * nz + z) * nt + t for z in range(nz)] for y in range(ny)]
        else:
            groups += [[(y * nz + z) * nt + t for y in range(ny)] for z in range(nz)]
    return groups


def swap(x, groups):
    return lax.all_to_all(x, PLANE, split_axis=0, concat_axis=0, axis_index_groups=groups, tiled=True)


def classes(first):
    return [line[parity::2] for line in lines(first) for parity in range(2)]


def mirror(x, first):
    pairs = [(line[i], line[i ^ 1]) for line in lines(first) for i in range(len(line))]
    return lax.ppermute(x, PLANE, pairs)


def dot(a, b, dims):
    return lax.dot_general(a, b, (dims, ((), ())), preferred_element_type=jnp.float32)


def live_mask(ids_ref, cnt_ref, tokens, ctx):
    row = lax.broadcasted_iota(jnp.int32, (tokens, ctx), 0) // BLK
    col = lax.broadcasted_iota(jnp.int32, (tokens, ctx), 1) // BLK
    live = None
    for b in range(tokens // BLK):
        for k in range(ids_ref.shape[2]):
            block = jnp.where(k < cnt_ref[0, b], ids_ref[0, b, k], -1)
            here = (row == b) & (col == block)
            live = here if live is None else live | here
    return live


def softmax(q, k, live):
    score = jnp.where(live, dot(q, k, ((1,), (1,))) * SCALE, jnp.float32(-1e30))
    expo = jnp.exp(score - jnp.max(score, axis=1, keepdims=True))
    return expo / jnp.sum(expo, axis=1, keepdims=True)


def forward_kernel(
    ids_hbm, cnt_hbm, q_hbm, kv_hbm, cot_hbm, keep_hbm, send_hbm,
    ids_ref, cnt_ref, q_ref, kv_ref, cot_ref, attn_ref, part_ref, sem, out_sem,
):
    copies = [
        pltpu.make_async_copy(src, dst, sem.at[i])
        for i, (src, dst) in enumerate(
            [(ids_hbm, ids_ref), (cnt_hbm, cnt_ref), (q_hbm, q_ref), (kv_hbm, kv_ref), (cot_hbm, cot_ref)]
        )
    ]
    for copy in copies:
        copy.start()
    tokens, width = q_ref.shape[1:]
    for copy in copies[:4]:
        copy.wait()
    live = live_mask(ids_ref, cnt_ref, tokens, kv_ref.shape[2])
    for h in range(width // HD):
        cols = slice(h * HD, (h + 1) * HD)
        prob = softmax(q_ref[0, :, cols], kv_ref[0, 0, :, cols], live).astype(jnp.bfloat16)
        attn_ref[:, cols] = dot(prob, kv_ref[0, 1, :, cols], ((1,), (0,))).astype(jnp.bfloat16)
    copies[4].wait()
    _, _, side, rows, _ = part_ref.shape
    attn = attn_ref[...]
    odd = lax.axis_index("tensor") % 2 == 1
    place = jnp.where(odd, lax.axis_index(DP[0]), lax.axis_index(DP[1]))
    parity = place % 2
    for y in range(side):
        span = side * rows
        part = dot(cot_ref[0, :, y * span : (y + 1) * span], attn, ((0,), (0,)))
        for z in range(side):
            block = part[z * rows : (z + 1) * rows].astype(jnp.bfloat16)
            other = (jnp.where(odd, y, z) + parity) % 2
            part_ref[other, jnp.where(odd, y // 2, z // 2), jnp.where(odd, z, y)] = block
    outs = [
        pltpu.make_async_copy(part_ref.at[i], out, out_sem.at[i]) for i, out in enumerate((keep_hbm, send_hbm))
    ]
    for out in outs:
        out.start()
    for out in outs:
        out.wait()


def backward_kernel(
    ids_hbm, cnt_hbm, q_hbm, kv_hbm, cot_hbm, same_hbm, other_hbm, gq_ref, gkv_ref,
    ids_ref, cnt_ref, q_ref, kv_ref, cot_ref, rows_ref, sem, row_sem,
):
    copies = [
        pltpu.make_async_copy(src, dst, sem.at[i])
        for i, (src, dst) in enumerate(
            [(ids_hbm, ids_ref), (cnt_hbm, cnt_ref), (q_hbm, q_ref), (kv_hbm, kv_ref), (cot_hbm, cot_ref)]
        )
    ]
    for copy in copies:
        copy.start()
    odd = lax.axis_index("tensor") % 2 == 1
    placed = []
    for turned in range(2):
        parity = lax.axis_index(DP[1] if turned else DP[0]) % 2
        moves = []
        for n, half in enumerate((same_hbm, other_hbm)):
            for j in range(half.shape[0]):
                at = 2 * j + (parity + n) % 2
                target = rows_ref.at[:, at] if turned else rows_ref.at[at]
                moves.append(pltpu.make_async_copy(half.at[j], target, row_sem.at[n * half.shape[0] + j]))
        placed.append(moves)

        @pl.when(odd == (turned == 1))
        def _(moves=moves):
            for move in moves:
                move.start()

    tokens, width = q_ref.shape[1:]
    for copy in copies[:4]:
        copy.wait()
    live = live_mask(ids_ref, cnt_ref, tokens, kv_ref.shape[2])
    side, _, rows, _ = rows_ref.shape
    probs = []
    attns = []
    for h in range(width // HD):
        cols = slice(h * HD, (h + 1) * HD)
        prob = softmax(q_ref[0, :, cols], kv_ref[0, 0, :, cols], live)
        probs.append(prob)
        attns.append(
            dot(prob.astype(jnp.bfloat16), kv_ref[0, 1, :, cols], ((1,), (0,))).astype(jnp.bfloat16)
        )
    copies[4].wait()
    for move in placed[0]:
        move.wait()
    weight = rows_ref[...].reshape(side * side * rows, width)
    d_attn = dot(cot_ref[0], weight, ((1,), (0,))).astype(jnp.bfloat16)
    for h in range(width // HD):
        cols = slice(h * HD, (h + 1) * HD)
        da = d_attn[:, cols]
        q, k, v = q_ref[0, :, cols], kv_ref[0, 0, :, cols], kv_ref[0, 1, :, cols]
        prob = probs[h]
        delta = jnp.sum(da.astype(jnp.float32) * attns[h].astype(jnp.float32), axis=1, keepdims=True)
        dprob = dot(da, v, ((1,), (1,)))
        dscore = (prob * (dprob - delta)).astype(jnp.bfloat16)
        gq_ref[0, :, cols] = (dot(dscore, k, ((1,), (0,))) * SCALE).astype(jnp.bfloat16)
        gkv_ref[0, 0, :, cols] = (dot(dscore, q, ((0,), (0,))) * SCALE).astype(jnp.bfloat16)
        gkv_ref[0, 1, :, cols] = dot(prob.astype(jnp.bfloat16), da, ((0,), (0,))).astype(jnp.bfloat16)


def fold_kernel(parts_ref, total_ref):
    total = parts_ref[0].astype(jnp.float32)
    for i in range(1, parts_ref.shape[0]):
        total += parts_ref[i].astype(jnp.float32)
    total_ref[...] = total.astype(total_ref.dtype)


def fold(parts, dtype):
    vmem = pl.BlockSpec(memory_space=pltpu.VMEM)
    return pl.pallas_call(
        fold_kernel,
        name="fold",
        out_shape=jax.ShapeDtypeStruct(parts.shape[1:], dtype),
        in_specs=[vmem],
        out_specs=vmem,
        compiler_params=pltpu.CompilerParams(vmem_limit_bytes=VMEM_LIMIT),
        cost_estimate=pl.CostEstimate(flops=parts.size, bytes_accessed=2 * parts.size, transcendentals=0),
    )(parts)


def shards(queries, context, vis_blocks, vis_count, w_out, grad_out):
    tokens, width = queries.shape[1:]
    ctx = context.shape[2]
    heads = width // HD
    model = grad_out.shape[2]
    ny, nz = (lax.axis_size(a) for a in DP)
    rows = w_out.shape[1]
    hbm = pl.BlockSpec(memory_space=pltpu.HBM)
    anywhere = pl.BlockSpec(memory_space=pl.ANY)
    vmem = pl.BlockSpec(memory_space=pltpu.VMEM)
    params = pltpu.CompilerParams(vmem_limit_bytes=VMEM_LIMIT)
    small = [
        pltpu.SMEM(vis_blocks.shape, jnp.int32),
        pltpu.SMEM(vis_count.shape, jnp.int32),
        pltpu.VMEM(queries.shape, jnp.bfloat16),
        pltpu.VMEM(context.shape, jnp.bfloat16),
        pltpu.VMEM(grad_out.shape, jnp.bfloat16),
    ]

    used = from_behind(context, "segment", 1)
    near = swap(jnp.broadcast_to(w_out, (nz, rows, width)), lines(True))
    same = swap(jnp.broadcast_to(near[None], (ny // 2, nz, rows, width)), classes(False))
    other = mirror(same, False)
    fixed = [pltpu.with_memory_space_constraint(a, pltpu.HBM) for a in (vis_blocks, vis_count, queries)]
    cotan = pltpu.with_memory_space_constraint(grad_out, pltpu.HBM)

    half = jax.ShapeDtypeStruct((nz // 2, ny, rows, width), jnp.bfloat16)
    keep, send = pl.pallas_call(
        forward_kernel,
        name="forward",
        out_shape=(half, half),
        in_specs=[hbm, hbm, hbm, anywhere, hbm],
        out_specs=(anywhere, anywhere),
        scratch_shapes=small
        + [
            pltpu.VMEM((tokens, width), jnp.bfloat16),
            pltpu.VMEM((2, *half.shape), jnp.bfloat16),
            pltpu.SemaphoreType.DMA((5,)),
            pltpu.SemaphoreType.DMA((2,)),
        ],
        compiler_params=params,
        cost_estimate=pl.CostEstimate(
            flops=2 * tokens * width * (2 * ctx + model), bytes_accessed=3 << 20, transcendentals=heads * tokens * ctx
        ),
    )(*fixed, used, cotan)

    pair = keep.astype(jnp.float32) + mirror(send, True).astype(jnp.float32)
    once = fold(swap(pair.astype(jnp.bfloat16), classes(True)), jnp.bfloat16)
    grad_weight = fold(swap(once, lines(False)), jnp.float32)[None]

    grad_q, grad_used = pl.pallas_call(
        backward_kernel,
        name="backward",
        out_shape=(
            jax.ShapeDtypeStruct(queries.shape, jnp.bfloat16),
            jax.ShapeDtypeStruct(context.shape, jnp.bfloat16),
        ),
        in_specs=[hbm, hbm, hbm, anywhere, hbm, anywhere, anywhere],
        out_specs=(vmem, vmem),
        scratch_shapes=small
        + [
            pltpu.VMEM((ny, nz, rows, width), jnp.bfloat16),
            pltpu.SemaphoreType.DMA((5,)),
            pltpu.SemaphoreType.DMA((ny,)),
        ],
        compiler_params=params,
        cost_estimate=pl.CostEstimate(
            flops=2 * tokens * width * (6 * ctx + model), bytes_accessed=4 << 20, transcendentals=heads * tokens * ctx
        ),
    )(*fixed, used, cotan, same, other)
    grad_context = from_behind(grad_used, "segment", -1)
    return grad_q, grad_context, grad_weight


def solution(mesh):
    fine = Mesh(mesh.devices.reshape(4, 8, 8, 4), ("segment", "y", "z", "tensor"))
    in_specs = (
        P("segment", DP, "tensor"),
        P("segment", None, DP, "tensor"),
        P("segment", DP, None),
        P("segment", DP),
        P("segment", DP, "tensor"),
        P("segment", DP, None),
    )
    out_specs = (
        P("segment", DP, "tensor"),
        P("segment", None, DP, "tensor"),
        P("segment", DP, "tensor"),
    )
    return jax.shard_map(shards, mesh=fine, in_specs=in_specs, out_specs=out_specs, check_vma=False)
```

```python
import jax
import jax.numpy as jnp
from jax import lax
from jax.experimental import pallas as pl
from jax.experimental.pallas import tpu as pltpu
from jax.sharding import Mesh, PartitionSpec as P

HD = 128
BLK = 128
VMEM_LIMIT = 16 * 1024 * 1024
SCALE = 1.0 / HD**0.5
DP = ("y", "z")
PLANE = ("y", "z", "tensor")


def from_behind(x, axis, by):
    count = lax.axis_size(axis)
    return lax.ppermute(x, axis, [(i, (i + by) % count) for i in range(count)])


def lines(first):
    ny, nz, nt = (lax.axis_size(a) for a in PLANE)
    groups = []
    for t in range(nt):
        if (t % 2 == 0) == first:
            groups += [[(y * nz + z) * nt + t for z in range(nz)] for y in range(ny)]
        else:
            groups += [[(y * nz + z) * nt + t for y in range(ny)] for z in range(nz)]
    return groups


def swap(x, first):
    return lax.all_to_all(
        x, PLANE, split_axis=0, concat_axis=0, axis_index_groups=lines(first), tiled=True
    )


def dot(a, b, dims):
    return lax.dot_general(a, b, (dims, ((), ())), preferred_element_type=jnp.float32)


def live_mask(ids_ref, cnt_ref, tokens, ctx):
    row = lax.broadcasted_iota(jnp.int32, (tokens, ctx), 0) // BLK
    col = lax.broadcasted_iota(jnp.int32, (tokens, ctx), 1) // BLK
    live = None
    for b in range(tokens // BLK):
        for k in range(ids_ref.shape[2]):
            block = jnp.where(k < cnt_ref[0, b], ids_ref[0, b, k], -1)
            here = (row == b) & (col == block)
            live = here if live is None else live | here
    return live


def softmax(q, k, live):
    score = jnp.where(live, dot(q, k, ((1,), (1,))) * SCALE, jnp.float32(-1e30))
    expo = jnp.exp(score - jnp.max(score, axis=1, keepdims=True))
    return expo / jnp.sum(expo, axis=1, keepdims=True)


def forward_kernel(
    ids_hbm, cnt_hbm, q_hbm, kv_hbm, cot_hbm, part_ref, ids_ref, cnt_ref, q_ref, kv_ref, cot_ref, attn_ref, sem
):
    copies = [
        pltpu.make_async_copy(src, dst, sem.at[i])
        for i, (src, dst) in enumerate(
            [(ids_hbm, ids_ref), (cnt_hbm, cnt_ref), (q_hbm, q_ref), (kv_hbm, kv_ref), (cot_hbm, cot_ref)]
        )
    ]
    for copy in copies:
        copy.start()
    tokens, width = q_ref.shape[1:]
    for copy in copies[:4]:
        copy.wait()
    live = live_mask(ids_ref, cnt_ref, tokens, kv_ref.shape[2])
    for h in range(width // HD):
        cols = slice(h * HD, (h + 1) * HD)
        prob = softmax(q_ref[0, :, cols], kv_ref[0, 0, :, cols], live).astype(jnp.bfloat16)
        attn_ref[:, cols] = dot(prob, kv_ref[0, 1, :, cols], ((1,), (0,))).astype(jnp.bfloat16)
    copies[4].wait()
    side, _, rows, _ = part_ref.shape
    attn = attn_ref[...]
    odd = lax.axis_index("tensor") % 2 == 1
    for y in range(side):
        span = side * rows
        part = dot(cot_ref[0, :, y * span : (y + 1) * span], attn, ((0,), (0,)))
        for z in range(side):
            block = part[z * rows : (z + 1) * rows].astype(jnp.bfloat16)
            part_ref[jnp.where(odd, y, z), jnp.where(odd, z, y)] = block


def backward_kernel(
    ids_hbm, cnt_hbm, q_hbm, kv_hbm, cot_hbm, far_hbm, gq_ref, gkv_ref,
    ids_ref, cnt_ref, q_ref, kv_ref, cot_ref, rows_ref, sem, row_sem,
):
    copies = [
        pltpu.make_async_copy(src, dst, sem.at[i])
        for i, (src, dst) in enumerate(
            [(ids_hbm, ids_ref), (cnt_hbm, cnt_ref), (q_hbm, q_ref), (kv_hbm, kv_ref), (cot_hbm, cot_ref)]
        )
    ]
    for copy in copies:
        copy.start()
    odd = lax.axis_index("tensor") % 2 == 1
    side, _, rows, _ = rows_ref.shape
    moves = [
        [
            pltpu.make_async_copy(
                far_hbm.at[:, y] if turned else far_hbm.at[y], rows_ref.at[y], row_sem.at[y]
            )
            for y in range(side)
        ]
        for turned in range(2)
    ]
    for turned in range(2):

        @pl.when(odd == (turned == 1))
        def _(turned=turned):
            for move in moves[turned]:
                move.start()

    tokens, width = q_ref.shape[1:]
    for copy in copies[:4]:
        copy.wait()
    live = live_mask(ids_ref, cnt_ref, tokens, kv_ref.shape[2])
    probs = []
    attns = []
    for h in range(width // HD):
        cols = slice(h * HD, (h + 1) * HD)
        prob = softmax(q_ref[0, :, cols], kv_ref[0, 0, :, cols], live)
        probs.append(prob)
        attns.append(
            dot(prob.astype(jnp.bfloat16), kv_ref[0, 1, :, cols], ((1,), (0,))).astype(jnp.bfloat16)
        )
    copies[4].wait()
    for move in moves[0]:
        move.wait()
    weight = rows_ref[...].reshape(side * side * rows, width)
    d_attn = dot(cot_ref[0], weight, ((1,), (0,))).astype(jnp.bfloat16)
    for h in range(width // HD):
        cols = slice(h * HD, (h + 1) * HD)
        da = d_attn[:, cols]
        q, k, v = q_ref[0, :, cols], kv_ref[0, 0, :, cols], kv_ref[0, 1, :, cols]
        prob = probs[h]
        delta = jnp.sum(da.astype(jnp.float32) * attns[h].astype(jnp.float32), axis=1, keepdims=True)
        dprob = dot(da, v, ((1,), (1,)))
        dscore = (prob * (dprob - delta)).astype(jnp.bfloat16)
        gq_ref[0, :, cols] = (dot(dscore, k, ((1,), (0,))) * SCALE).astype(jnp.bfloat16)
        gkv_ref[0, 0, :, cols] = (dot(dscore, q, ((0,), (0,))) * SCALE).astype(jnp.bfloat16)
        gkv_ref[0, 1, :, cols] = dot(prob.astype(jnp.bfloat16), da, ((0,), (0,))).astype(jnp.bfloat16)


def fold_kernel(parts_ref, total_ref):
    total = parts_ref[0].astype(jnp.float32)
    for i in range(1, parts_ref.shape[0]):
        total += parts_ref[i].astype(jnp.float32)
    total_ref[...] = total.astype(total_ref.dtype)


def fold(parts, dtype):
    vmem = pl.BlockSpec(memory_space=pltpu.VMEM)
    return pl.pallas_call(
        fold_kernel,
        name="fold",
        out_shape=jax.ShapeDtypeStruct(parts.shape[1:], dtype),
        in_specs=[vmem],
        out_specs=vmem,
        compiler_params=pltpu.CompilerParams(vmem_limit_bytes=VMEM_LIMIT),
        cost_estimate=pl.CostEstimate(flops=parts.size, bytes_accessed=2 * parts.size, transcendentals=0),
    )(parts)


def shards(queries, context, vis_blocks, vis_count, w_out, grad_out):
    tokens, width = queries.shape[1:]
    ctx = context.shape[2]
    heads = width // HD
    model = grad_out.shape[2]
    ny, nz = (lax.axis_size(a) for a in DP)
    rows = w_out.shape[1]
    hbm = pl.BlockSpec(memory_space=pltpu.HBM)
    anywhere = pl.BlockSpec(memory_space=pl.ANY)
    vmem = pl.BlockSpec(memory_space=pltpu.VMEM)
    params = pltpu.CompilerParams(vmem_limit_bytes=VMEM_LIMIT)
    small = [
        pltpu.SMEM(vis_blocks.shape, jnp.int32),
        pltpu.SMEM(vis_count.shape, jnp.int32),
        pltpu.VMEM(queries.shape, jnp.bfloat16),
        pltpu.VMEM(context.shape, jnp.bfloat16),
        pltpu.VMEM(grad_out.shape, jnp.bfloat16),
    ]

    used = from_behind(context, "segment", 1)
    near = swap(jnp.broadcast_to(w_out, (nz, rows, width)), True)
    near, used = lax.optimization_barrier((near, used))
    far = swap(jnp.broadcast_to(near[None], (ny, nz, rows, width)), False)
    fixed = [pltpu.with_memory_space_constraint(a, pltpu.HBM) for a in (vis_blocks, vis_count, queries)]
    cotan = pltpu.with_memory_space_constraint(grad_out, pltpu.HBM)

    part = pl.pallas_call(
        forward_kernel,
        name="forward",
        out_shape=jax.ShapeDtypeStruct((nz, ny, rows, width), jnp.bfloat16),
        in_specs=[hbm, hbm, hbm, anywhere, hbm],
        out_specs=vmem,
        scratch_shapes=small + [pltpu.VMEM((tokens, width), jnp.bfloat16), pltpu.SemaphoreType.DMA((5,))],
        compiler_params=params,
        cost_estimate=pl.CostEstimate(
            flops=2 * tokens * width * (2 * ctx + model), bytes_accessed=3 << 20, transcendentals=heads * tokens * ctx
        ),
    )(*fixed, used, cotan)

    once = fold(swap(part, True), jnp.bfloat16)
    grad_weight = fold(swap(once, False), jnp.float32)[None]

    grad_q, grad_used = pl.pallas_call(
        backward_kernel,
        name="backward",
        out_shape=(
            jax.ShapeDtypeStruct(queries.shape, jnp.bfloat16),
            jax.ShapeDtypeStruct(context.shape, jnp.bfloat16),
        ),
        in_specs=[hbm, hbm, hbm, anywhere, hbm] + [anywhere],
        out_specs=(vmem, vmem),
        scratch_shapes=small
        + [
            pltpu.VMEM((ny, nz, rows, width), jnp.bfloat16),
            pltpu.SemaphoreType.DMA((5,)),
            pltpu.SemaphoreType.DMA((ny,)),
        ],
        compiler_params=params,
        cost_estimate=pl.CostEstimate(
            flops=2 * tokens * width * (6 * ctx + model), bytes_accessed=4 << 20, transcendentals=heads * tokens * ctx
        ),
    )(*fixed, used, cotan, far)
    grad_context = from_behind(grad_used, "segment", -1)
    return grad_q, grad_context, grad_weight


def solution(mesh):
    fine = Mesh(mesh.devices.reshape(4, 8, 8, 4), ("segment", "y", "z", "tensor"))
    in_specs = (
        P("segment", DP, "tensor"),
        P("segment", None, DP, "tensor"),
        P("segment", DP, None),
        P("segment", DP),
        P("segment", DP, "tensor"),
        P("segment", DP, None),
    )
    out_specs = (
        P("segment", DP, "tensor"),
        P("segment", None, DP, "tensor"),
        P("segment", DP, "tensor"),
    )
    return jax.shard_map(shards, mesh=fine, in_specs=in_specs, out_specs=out_specs, check_vma=False)
```

```python
import jax
import jax.numpy as jnp
from jax import lax
from jax.experimental import pallas as pl
from jax.experimental.pallas import tpu as pltpu
from jax.sharding import Mesh, PartitionSpec as P

HD = 128
BLK = 128
VMEM_LIMIT = 16 * 1024 * 1024
SCALE = 1.0 / HD**0.5
DP = ("y", "z")
PLANE = ("y", "z", "tensor")


def from_behind(x, axis, by):
    count = lax.axis_size(axis)
    return lax.ppermute(x, axis, [(i, (i + by) % count) for i in range(count)])


def lines(first):
    ny, nz, nt = (lax.axis_size(a) for a in PLANE)
    groups = []
    for t in range(nt):
        if (t % 2 == 0) == first:
            groups += [[(y * nz + z) * nt + t for z in range(nz)] for y in range(ny)]
        else:
            groups += [[(y * nz + z) * nt + t for y in range(ny)] for z in range(nz)]
    return groups


def swap(x, groups):
    return lax.all_to_all(x, PLANE, split_axis=0, concat_axis=0, axis_index_groups=groups, tiled=True)


def mirror(x, distance):
    pairs = [(line[i], line[i ^ distance]) for line in lines(False) for i in range(len(line))]
    return lax.ppermute(x, PLANE, pairs)


def pairs_of_lines():
    alone = lines(True)
    return [alone[i] + alone[i + 1] for i in range(0, len(alone), 2)]


def dot(a, b, dims):
    return lax.dot_general(a, b, (dims, ((), ())), preferred_element_type=jnp.float32)


def live_mask(ids_ref, cnt_ref, tokens, ctx):
    row = lax.broadcasted_iota(jnp.int32, (tokens, ctx), 0) // BLK
    col = lax.broadcasted_iota(jnp.int32, (tokens, ctx), 1) // BLK
    live = None
    for b in range(tokens // BLK):
        for k in range(ids_ref.shape[2]):
            block = jnp.where(k < cnt_ref[0, b], ids_ref[0, b, k], -1)
            here = (row == b) & (col == block)
            live = here if live is None else live | here
    return live


def softmax(q, k, live):
    score = jnp.where(live, dot(q, k, ((1,), (1,))) * SCALE, jnp.float32(-1e30))
    expo = jnp.exp(score - jnp.max(score, axis=1, keepdims=True))
    return expo / jnp.sum(expo, axis=1, keepdims=True)


def forward_kernel(
    ids_hbm, cnt_hbm, q_hbm, kv_hbm, cot_hbm, part_ref, ids_ref, cnt_ref, q_ref, kv_ref, cot_ref, attn_ref, sem
):
    copies = [
        pltpu.make_async_copy(src, dst, sem.at[i])
        for i, (src, dst) in enumerate(
            [(ids_hbm, ids_ref), (cnt_hbm, cnt_ref), (q_hbm, q_ref), (kv_hbm, kv_ref), (cot_hbm, cot_ref)]
        )
    ]
    for copy in copies:
        copy.start()
    tokens, width = q_ref.shape[1:]
    for copy in copies[:4]:
        copy.wait()
    live = live_mask(ids_ref, cnt_ref, tokens, kv_ref.shape[2])
    for h in range(width // HD):
        cols = slice(h * HD, (h + 1) * HD)
        prob = softmax(q_ref[0, :, cols], kv_ref[0, 0, :, cols], live).astype(jnp.bfloat16)
        attn_ref[:, cols] = dot(prob, kv_ref[0, 1, :, cols], ((1,), (0,))).astype(jnp.bfloat16)
    copies[4].wait()
    side, _, rows, _ = part_ref.shape
    attn = attn_ref[...]
    odd = lax.axis_index("tensor") % 2 == 1
    for y in range(side):
        span = side * rows
        part = dot(cot_ref[0, :, y * span : (y + 1) * span], attn, ((0,), (0,)))
        for z in range(side):
            block = part[z * rows : (z + 1) * rows].astype(jnp.bfloat16)
            part_ref[jnp.where(odd, y, z), jnp.where(odd, z, y)] = block


def backward_kernel(ids_hbm, cnt_hbm, q_hbm, kv_hbm, cot_hbm, *refs):
    pieces = refs[:-10]
    gq_ref, gkv_ref, ids_ref, cnt_ref, q_ref, kv_ref, cot_ref, rows_ref, sem, slot_sem = refs[-10:]
    copies = [
        pltpu.make_async_copy(src, dst, sem.at[i])
        for i, (src, dst) in enumerate(
            [(ids_hbm, ids_ref), (cnt_hbm, cnt_ref), (q_hbm, q_ref), (kv_hbm, kv_ref), (cot_hbm, cot_ref)]
        )
    ]
    for copy in copies:
        copy.start()
    odd = lax.axis_index("tensor") % 2 == 1
    placed = []
    for turned in range(2):
        place = lax.axis_index(DP[1] if turned else DP[0]) // 2
        moves = []
        for k, piece in enumerate(pieces):
            for i in range(2):
                at = 2 * (place ^ k) + i
                target = rows_ref.at[:, at] if turned else rows_ref.at[at]
                moves.append(pltpu.make_async_copy(piece.at[i], target, slot_sem.at[2 * k + i]))
        placed.append(moves)

        @pl.when(odd == (turned == 1))
        def _(moves=moves):
            for move in moves:
                move.start()

    tokens, width = q_ref.shape[1:]
    for copy in copies[:4]:
        copy.wait()
    live = live_mask(ids_ref, cnt_ref, tokens, kv_ref.shape[2])
    side, _, rows, _ = rows_ref.shape
    probs = []
    attns = []
    for h in range(width // HD):
        cols = slice(h * HD, (h + 1) * HD)
        prob = softmax(q_ref[0, :, cols], kv_ref[0, 0, :, cols], live)
        probs.append(prob)
        attns.append(
            dot(prob.astype(jnp.bfloat16), kv_ref[0, 1, :, cols], ((1,), (0,))).astype(jnp.bfloat16)
        )
    copies[4].wait()
    for move in placed[0]:
        move.wait()
    weight = rows_ref[...].reshape(side * side * rows, width)
    d_attn = dot(cot_ref[0], weight, ((1,), (0,))).astype(jnp.bfloat16)
    for h in range(width // HD):
        cols = slice(h * HD, (h + 1) * HD)
        da = d_attn[:, cols]
        q, k, v = q_ref[0, :, cols], kv_ref[0, 0, :, cols], kv_ref[0, 1, :, cols]
        prob = probs[h]
        delta = jnp.sum(da.astype(jnp.float32) * attns[h].astype(jnp.float32), axis=1, keepdims=True)
        dprob = dot(da, v, ((1,), (1,)))
        dscore = (prob * (dprob - delta)).astype(jnp.bfloat16)
        gq_ref[0, :, cols] = (dot(dscore, k, ((1,), (0,))) * SCALE).astype(jnp.bfloat16)
        gkv_ref[0, 0, :, cols] = (dot(dscore, q, ((0,), (0,))) * SCALE).astype(jnp.bfloat16)
        gkv_ref[0, 1, :, cols] = dot(prob.astype(jnp.bfloat16), da, ((0,), (0,))).astype(jnp.bfloat16)


def fold_kernel(parts_ref, total_ref):
    total = parts_ref[0].astype(jnp.float32)
    for i in range(1, parts_ref.shape[0]):
        total += parts_ref[i].astype(jnp.float32)
    total_ref[...] = total.astype(total_ref.dtype)


def fold(parts, dtype):
    vmem = pl.BlockSpec(memory_space=pltpu.VMEM)
    return pl.pallas_call(
        fold_kernel,
        name="fold",
        out_shape=jax.ShapeDtypeStruct(parts.shape[1:], dtype),
        in_specs=[vmem],
        out_specs=vmem,
        compiler_params=pltpu.CompilerParams(vmem_limit_bytes=VMEM_LIMIT),
        cost_estimate=pl.CostEstimate(flops=parts.size, bytes_accessed=2 * parts.size, transcendentals=0),
    )(parts)


def shards(queries, context, vis_blocks, vis_count, w_out, grad_out):
    tokens, width = queries.shape[1:]
    ctx = context.shape[2]
    heads = width // HD
    model = grad_out.shape[2]
    ny, nz = (lax.axis_size(a) for a in DP)
    rows = w_out.shape[1]
    hbm = pl.BlockSpec(memory_space=pltpu.HBM)
    anywhere = pl.BlockSpec(memory_space=pl.ANY)
    vmem = pl.BlockSpec(memory_space=pltpu.VMEM)
    params = pltpu.CompilerParams(vmem_limit_bytes=VMEM_LIMIT)
    small = [
        pltpu.SMEM(vis_blocks.shape, jnp.int32),
        pltpu.SMEM(vis_count.shape, jnp.int32),
        pltpu.VMEM(queries.shape, jnp.bfloat16),
        pltpu.VMEM(context.shape, jnp.bfloat16),
        pltpu.VMEM(grad_out.shape, jnp.bfloat16),
    ]

    used = from_behind(context, "segment", 1)
    near = swap(jnp.broadcast_to(w_out, (2 * nz, rows, width)), pairs_of_lines())
    fixed = [pltpu.with_memory_space_constraint(a, pltpu.HBM) for a in (vis_blocks, vis_count, queries)]
    cotan = pltpu.with_memory_space_constraint(grad_out, pltpu.HBM)

    part = pl.pallas_call(
        forward_kernel,
        name="forward",
        out_shape=jax.ShapeDtypeStruct((nz, ny, rows, width), jnp.bfloat16),
        in_specs=[hbm, hbm, hbm, anywhere, hbm],
        out_specs=vmem,
        scratch_shapes=small + [pltpu.VMEM((tokens, width), jnp.bfloat16), pltpu.SemaphoreType.DMA((5,))],
        compiler_params=params,
        cost_estimate=pl.CostEstimate(
            flops=2 * tokens * width * (2 * ctx + model), bytes_accessed=3 << 20, transcendentals=heads * tokens * ctx
        ),
    )(*fixed, used, cotan)

    once = fold(swap(part, lines(True)), jnp.bfloat16)
    grad_weight = fold(swap(once, lines(False)), jnp.float32)[None]

    pair = near.reshape(2, nz, rows, width)
    pieces = [pair] + [mirror(pair, k) for k in range(2, ny, 2)]
    grad_q, grad_used = pl.pallas_call(
        backward_kernel,
        name="backward",
        out_shape=(
            jax.ShapeDtypeStruct(queries.shape, jnp.bfloat16),
            jax.ShapeDtypeStruct(context.shape, jnp.bfloat16),
        ),
        in_specs=[hbm, hbm, hbm, anywhere, hbm] + [anywhere] * len(pieces),
        out_specs=(vmem, vmem),
        scratch_shapes=small
        + [
            pltpu.VMEM((ny, nz, rows, width), jnp.bfloat16),
            pltpu.SemaphoreType.DMA((5,)),
            pltpu.SemaphoreType.DMA((ny,)),
        ],
        compiler_params=params,
        cost_estimate=pl.CostEstimate(
            flops=2 * tokens * width * (6 * ctx + model), bytes_accessed=4 << 20, transcendentals=heads * tokens * ctx
        ),
    )(*fixed, used, cotan, *pieces)
    grad_context = from_behind(grad_used, "segment", -1)
    return grad_q, grad_context, grad_weight


def solution(mesh):
    fine = Mesh(mesh.devices.reshape(4, 8, 8, 4), ("segment", "y", "z", "tensor"))
    in_specs = (
        P("segment", DP, "tensor"),
        P("segment", None, DP, "tensor"),
        P("segment", DP, None),
        P("segment", DP),
        P("segment", DP, "tensor"),
        P("segment", DP, None),
    )
    out_specs = (
        P("segment", DP, "tensor"),
        P("segment", None, DP, "tensor"),
        P("segment", DP, "tensor"),
    )
    return jax.shard_map(shards, mesh=fine, in_specs=in_specs, out_specs=out_specs, check_vma=False)
```

```python
import jax
import jax.numpy as jnp
from jax import lax
from jax.experimental import pallas as pl
from jax.experimental.pallas import tpu as pltpu
from jax.sharding import Mesh, PartitionSpec as P

HD = 128
BLK = 128
VMEM_LIMIT = 16 * 1024 * 1024
SCALE = 1.0 / HD**0.5
DP = ("y", "z")
PLANE = ("y", "z", "tensor")


def from_behind(x, axis, by):
    count = lax.axis_size(axis)
    return lax.ppermute(x, axis, [(i, (i + by) % count) for i in range(count)])


def lines(first):
    ny, nz, nt = (lax.axis_size(a) for a in PLANE)
    groups = []
    for t in range(nt):
        if (t % 2 == 0) == first:
            groups += [[(y * nz + z) * nt + t for z in range(nz)] for y in range(ny)]
        else:
            groups += [[(y * nz + z) * nt + t for y in range(ny)] for z in range(nz)]
    return groups


def swap(x, first):
    return lax.all_to_all(
        x, PLANE, split_axis=0, concat_axis=0, axis_index_groups=lines(first), tiled=True
    )


def dot(a, b, dims):
    return lax.dot_general(a, b, (dims, ((), ())), preferred_element_type=jnp.float32)


def live_mask(ids_ref, cnt_ref, tokens, ctx):
    row = lax.broadcasted_iota(jnp.int32, (tokens, ctx), 0) // BLK
    col = lax.broadcasted_iota(jnp.int32, (tokens, ctx), 1) // BLK
    live = None
    for b in range(tokens // BLK):
        for k in range(ids_ref.shape[2]):
            block = jnp.where(k < cnt_ref[0, b], ids_ref[0, b, k], -1)
            here = (row == b) & (col == block)
            live = here if live is None else live | here
    return live


def softmax(q, k, live):
    score = jnp.where(live, dot(q, k, ((1,), (1,))) * SCALE, jnp.float32(-1e30))
    expo = jnp.exp(score - jnp.max(score, axis=1, keepdims=True))
    return expo / jnp.sum(expo, axis=1, keepdims=True)


def forward_kernel(
    ids_hbm, cnt_hbm, q_hbm, kv_hbm, cot_hbm, part_ref, ids_ref, cnt_ref, q_ref, kv_ref, cot_ref, attn_ref, sem
):
    copies = [
        pltpu.make_async_copy(src, dst, sem.at[i])
        for i, (src, dst) in enumerate(
            [(ids_hbm, ids_ref), (cnt_hbm, cnt_ref), (q_hbm, q_ref), (kv_hbm, kv_ref), (cot_hbm, cot_ref)]
        )
    ]
    for copy in copies:
        copy.start()
    tokens, width = q_ref.shape[1:]
    for copy in copies[:4]:
        copy.wait()
    live = live_mask(ids_ref, cnt_ref, tokens, kv_ref.shape[2])
    for h in range(width // HD):
        cols = slice(h * HD, (h + 1) * HD)
        prob = softmax(q_ref[0, :, cols], kv_ref[0, 0, :, cols], live).astype(jnp.bfloat16)
        attn_ref[:, cols] = dot(prob, kv_ref[0, 1, :, cols], ((1,), (0,))).astype(jnp.bfloat16)
    copies[4].wait()
    side, _, rows, _ = part_ref.shape
    attn = attn_ref[...]
    odd = lax.axis_index("tensor") % 2 == 1
    for y in range(side):
        span = side * rows
        part = dot(cot_ref[0, :, y * span : (y + 1) * span], attn, ((0,), (0,)))
        for z in range(side):
            block = part[z * rows : (z + 1) * rows].astype(jnp.bfloat16)
            part_ref[jnp.where(odd, y, z), jnp.where(odd, z, y)] = block


def backward_kernel(
    ids_hbm, cnt_hbm, q_hbm, kv_hbm, cot_hbm, far_hbm, gq_ref, gkv_ref,
    ids_ref, cnt_ref, q_ref, kv_ref, cot_ref, rows_ref, sem, row_sem,
):
    copies = [
        pltpu.make_async_copy(src, dst, sem.at[i])
        for i, (src, dst) in enumerate(
            [(ids_hbm, ids_ref), (cnt_hbm, cnt_ref), (q_hbm, q_ref), (kv_hbm, kv_ref), (cot_hbm, cot_ref)]
        )
    ]
    for copy in copies:
        copy.start()
    odd = lax.axis_index("tensor") % 2 == 1
    side, _, rows, _ = rows_ref.shape
    moves = [
        [
            pltpu.make_async_copy(
                far_hbm.at[:, y] if turned else far_hbm.at[y], rows_ref.at[y], row_sem.at[y]
            )
            for y in range(side)
        ]
        for turned in range(2)
    ]
    for turned in range(2):

        @pl.when(odd == (turned == 1))
        def _(turned=turned):
            for move in moves[turned]:
                move.start()

    tokens, width = q_ref.shape[1:]
    for copy in copies[:4]:
        copy.wait()
    live = live_mask(ids_ref, cnt_ref, tokens, kv_ref.shape[2])
    probs = []
    attns = []
    for h in range(width // HD):
        cols = slice(h * HD, (h + 1) * HD)
        prob = softmax(q_ref[0, :, cols], kv_ref[0, 0, :, cols], live)
        probs.append(prob)
        attns.append(
            dot(prob.astype(jnp.bfloat16), kv_ref[0, 1, :, cols], ((1,), (0,))).astype(jnp.bfloat16)
        )
    copies[4].wait()
    for move in moves[0]:
        move.wait()
    weight = rows_ref[...].reshape(side * side * rows, width)
    d_attn = dot(cot_ref[0], weight, ((1,), (0,))).astype(jnp.bfloat16)
    for h in range(width // HD):
        cols = slice(h * HD, (h + 1) * HD)
        da = d_attn[:, cols]
        q, k, v = q_ref[0, :, cols], kv_ref[0, 0, :, cols], kv_ref[0, 1, :, cols]
        prob = probs[h]
        delta = jnp.sum(da.astype(jnp.float32) * attns[h].astype(jnp.float32), axis=1, keepdims=True)
        dprob = dot(da, v, ((1,), (1,)))
        dscore = (prob * (dprob - delta)).astype(jnp.bfloat16)
        gq_ref[0, :, cols] = (dot(dscore, k, ((1,), (0,))) * SCALE).astype(jnp.bfloat16)
        gkv_ref[0, 0, :, cols] = (dot(dscore, q, ((0,), (0,))) * SCALE).astype(jnp.bfloat16)
        gkv_ref[0, 1, :, cols] = dot(prob.astype(jnp.bfloat16), da, ((0,), (0,))).astype(jnp.bfloat16)


def fold_kernel(parts_ref, total_ref):
    total = parts_ref[0].astype(jnp.float32)
    for i in range(1, parts_ref.shape[0]):
        total += parts_ref[i].astype(jnp.float32)
    total_ref[...] = total.astype(total_ref.dtype)


def fold(parts, dtype):
    vmem = pl.BlockSpec(memory_space=pltpu.VMEM)
    return pl.pallas_call(
        fold_kernel,
        name="fold",
        out_shape=jax.ShapeDtypeStruct(parts.shape[1:], dtype),
        in_specs=[vmem],
        out_specs=vmem,
        compiler_params=pltpu.CompilerParams(vmem_limit_bytes=VMEM_LIMIT),
        cost_estimate=pl.CostEstimate(flops=parts.size, bytes_accessed=2 * parts.size, transcendentals=0),
    )(parts)


def shards(queries, context, vis_blocks, vis_count, w_out, grad_out):
    tokens, width = queries.shape[1:]
    ctx = context.shape[2]
    heads = width // HD
    model = grad_out.shape[2]
    ny, nz = (lax.axis_size(a) for a in DP)
    rows = w_out.shape[1]
    hbm = pl.BlockSpec(memory_space=pltpu.HBM)
    anywhere = pl.BlockSpec(memory_space=pl.ANY)
    vmem = pl.BlockSpec(memory_space=pltpu.VMEM)
    params = pltpu.CompilerParams(vmem_limit_bytes=VMEM_LIMIT)
    small = [
        pltpu.SMEM(vis_blocks.shape, jnp.int32),
        pltpu.SMEM(vis_count.shape, jnp.int32),
        pltpu.VMEM(queries.shape, jnp.bfloat16),
        pltpu.VMEM(context.shape, jnp.bfloat16),
        pltpu.VMEM(grad_out.shape, jnp.bfloat16),
    ]

    used = from_behind(context, "segment", 1)
    near = swap(jnp.broadcast_to(w_out, (nz, rows, width)), True)
    fixed = [pltpu.with_memory_space_constraint(a, pltpu.HBM) for a in (vis_blocks, vis_count, queries)]
    cotan = pltpu.with_memory_space_constraint(grad_out, pltpu.HBM)

    part = pl.pallas_call(
        forward_kernel,
        name="forward",
        out_shape=jax.ShapeDtypeStruct((nz, ny, rows, width), jnp.bfloat16),
        in_specs=[hbm, hbm, hbm, anywhere, hbm],
        out_specs=vmem,
        scratch_shapes=small + [pltpu.VMEM((tokens, width), jnp.bfloat16), pltpu.SemaphoreType.DMA((5,))],
        compiler_params=params,
        cost_estimate=pl.CostEstimate(
            flops=2 * tokens * width * (2 * ctx + model), bytes_accessed=3 << 20, transcendentals=heads * tokens * ctx
        ),
    )(*fixed, used, cotan)

    once = fold(swap(part, True), jnp.bfloat16)
    grad_weight = fold(swap(once, False), jnp.float32)[None]

    far = swap(jnp.broadcast_to(near[None], (ny, nz, rows, width)), False)
    grad_q, grad_used = pl.pallas_call(
        backward_kernel,
        name="backward",
        out_shape=(
            jax.ShapeDtypeStruct(queries.shape, jnp.bfloat16),
            jax.ShapeDtypeStruct(context.shape, jnp.bfloat16),
        ),
        in_specs=[hbm, hbm, hbm, anywhere, hbm] + [anywhere],
        out_specs=(vmem, vmem),
        scratch_shapes=small
        + [
            pltpu.VMEM((ny, nz, rows, width), jnp.bfloat16),
            pltpu.SemaphoreType.DMA((5,)),
            pltpu.SemaphoreType.DMA((ny,)),
        ],
        compiler_params=params,
        cost_estimate=pl.CostEstimate(
            flops=2 * tokens * width * (6 * ctx + model), bytes_accessed=4 << 20, transcendentals=heads * tokens * ctx
        ),
    )(*fixed, used, cotan, far)
    grad_context = from_behind(grad_used, "segment", -1)
    return grad_q, grad_context, grad_weight


def solution(mesh):
    fine = Mesh(mesh.devices.reshape(4, 8, 8, 4), ("segment", "y", "z", "tensor"))
    in_specs = (
        P("segment", DP, "tensor"),
        P("segment", None, DP, "tensor"),
        P("segment", DP, None),
        P("segment", DP),
        P("segment", DP, "tensor"),
        P("segment", DP, None),
    )
    out_specs = (
        P("segment", DP, "tensor"),
        P("segment", None, DP, "tensor"),
        P("segment", DP, "tensor"),
    )
    return jax.shard_map(shards, mesh=fine, in_specs=in_specs, out_specs=out_specs, check_vma=False)
```

```python
import jax
import jax.numpy as jnp
from jax import lax
from jax.experimental import pallas as pl
from jax.experimental.pallas import tpu as pltpu
from jax.sharding import Mesh, PartitionSpec as P

HD = 128
BLK = 128
VMEM_LIMIT = 16 * 1024 * 1024
SCALE = 1.0 / HD**0.5
DP = ("y", "z")
PLANE = ("y", "z", "tensor")


def from_behind(x, axis, by):
    count = lax.axis_size(axis)
    return lax.ppermute(x, axis, [(i, (i + by) % count) for i in range(count)])


def lines(first):
    ny, nz, nt = (lax.axis_size(a) for a in PLANE)
    groups = []
    for t in range(nt):
        if (t % 2 == 0) == first:
            groups += [[(y * nz + z) * nt + t for z in range(nz)] for y in range(ny)]
        else:
            groups += [[(y * nz + z) * nt + t for y in range(ny)] for z in range(nz)]
    return groups


def swap(x, first):
    return lax.all_to_all(
        x, PLANE, split_axis=0, concat_axis=0, axis_index_groups=lines(first), tiled=True
    )


def dot(a, b, dims):
    return lax.dot_general(a, b, (dims, ((), ())), preferred_element_type=jnp.float32)


def live_mask(ids_ref, cnt_ref, tokens, ctx):
    row = lax.broadcasted_iota(jnp.int32, (tokens, ctx), 0) // BLK
    col = lax.broadcasted_iota(jnp.int32, (tokens, ctx), 1) // BLK
    live = None
    for b in range(tokens // BLK):
        for k in range(ids_ref.shape[2]):
            block = jnp.where(k < cnt_ref[0, b], ids_ref[0, b, k], -1)
            here = (row == b) & (col == block)
            live = here if live is None else live | here
    return live


def softmax(q, k, live):
    score = jnp.where(live, dot(q, k, ((1,), (1,))) * SCALE, jnp.float32(-1e30))
    expo = jnp.exp(score - jnp.max(score, axis=1, keepdims=True))
    return expo / jnp.sum(expo, axis=1, keepdims=True)


def forward_kernel(
    ids_hbm, cnt_hbm, q_hbm, kv_hbm, cot_hbm, part_ref, ids_ref, cnt_ref, q_ref, kv_ref, cot_ref, attn_ref, sem
):
    copies = [
        pltpu.make_async_copy(src, dst, sem.at[i])
        for i, (src, dst) in enumerate(
            [(ids_hbm, ids_ref), (cnt_hbm, cnt_ref), (q_hbm, q_ref), (kv_hbm, kv_ref), (cot_hbm, cot_ref)]
        )
    ]
    for copy in copies:
        copy.start()
    tokens, width = q_ref.shape[1:]
    for copy in copies[:4]:
        copy.wait()
    live = live_mask(ids_ref, cnt_ref, tokens, kv_ref.shape[2])
    for h in range(width // HD):
        cols = slice(h * HD, (h + 1) * HD)
        prob = softmax(q_ref[0, :, cols], kv_ref[0, 0, :, cols], live).astype(jnp.bfloat16)
        attn_ref[:, cols] = dot(prob, kv_ref[0, 1, :, cols], ((1,), (0,))).astype(jnp.bfloat16)
    copies[4].wait()
    side, _, rows, _ = part_ref.shape
    attn = attn_ref[...]
    odd = lax.axis_index("tensor") % 2 == 1
    for y in range(side):
        span = side * rows
        part = dot(cot_ref[0, :, y * span : (y + 1) * span], attn, ((0,), (0,)))
        for z in range(side):
            block = part[z * rows : (z + 1) * rows].astype(jnp.bfloat16)
            part_ref[jnp.where(odd, y, z), jnp.where(odd, z, y)] = block


def backward_kernel(
    ids_hbm, cnt_hbm, q_hbm, kv_hbm, cot_hbm, far_hbm, gq_ref, gkv_ref,
    ids_ref, cnt_ref, q_ref, kv_ref, cot_ref, rows_ref, sem, row_sem,
):
    copies = [
        pltpu.make_async_copy(src, dst, sem.at[i])
        for i, (src, dst) in enumerate(
            [(ids_hbm, ids_ref), (cnt_hbm, cnt_ref), (q_hbm, q_ref), (kv_hbm, kv_ref), (cot_hbm, cot_ref)]
        )
    ]
    for copy in copies:
        copy.start()
    odd = lax.axis_index("tensor") % 2 == 1
    side, _, rows, _ = rows_ref.shape
    moves = [
        [
            pltpu.make_async_copy(
                far_hbm.at[:, y] if turned else far_hbm.at[y], rows_ref.at[y], row_sem.at[y]
            )
            for y in range(side)
        ]
        for turned in range(2)
    ]
    for turned in range(2):

        @pl.when(odd == (turned == 1))
        def _(turned=turned):
            for move in moves[turned]:
                move.start()

    tokens, width = q_ref.shape[1:]
    for copy in copies[:4]:
        copy.wait()
    live = live_mask(ids_ref, cnt_ref, tokens, kv_ref.shape[2])
    probs = []
    attns = []
    for h in range(width // HD):
        cols = slice(h * HD, (h + 1) * HD)
        prob = softmax(q_ref[0, :, cols], kv_ref[0, 0, :, cols], live)
        probs.append(prob)
        attns.append(
            dot(prob.astype(jnp.bfloat16), kv_ref[0, 1, :, cols], ((1,), (0,))).astype(jnp.bfloat16)
        )
    copies[4].wait()
    for move in moves[0]:
        move.wait()
    weight = rows_ref[...].reshape(side * side * rows, width)
    d_attn = dot(cot_ref[0], weight, ((1,), (0,))).astype(jnp.bfloat16)
    for h in range(width // HD):
        cols = slice(h * HD, (h + 1) * HD)
        da = d_attn[:, cols]
        q, k, v = q_ref[0, :, cols], kv_ref[0, 0, :, cols], kv_ref[0, 1, :, cols]
        prob = probs[h]
        delta = jnp.sum(da.astype(jnp.float32) * attns[h].astype(jnp.float32), axis=1, keepdims=True)
        dprob = dot(da, v, ((1,), (1,)))
        dscore = (prob * (dprob - delta)).astype(jnp.bfloat16)
        gq_ref[0, :, cols] = (dot(dscore, k, ((1,), (0,))) * SCALE).astype(jnp.bfloat16)
        gkv_ref[0, 0, :, cols] = (dot(dscore, q, ((0,), (0,))) * SCALE).astype(jnp.bfloat16)
        gkv_ref[0, 1, :, cols] = dot(prob.astype(jnp.bfloat16), da, ((0,), (0,))).astype(jnp.bfloat16)


def fold_kernel(parts_ref, total_ref):
    total = parts_ref[0].astype(jnp.float32)
    for i in range(1, parts_ref.shape[0]):
        total += parts_ref[i].astype(jnp.float32)
    total_ref[...] = total.astype(total_ref.dtype)


def fold(parts, dtype):
    vmem = pl.BlockSpec(memory_space=pltpu.VMEM)
    return pl.pallas_call(
        fold_kernel,
        name="fold",
        out_shape=jax.ShapeDtypeStruct(parts.shape[1:], dtype),
        in_specs=[vmem],
        out_specs=vmem,
        compiler_params=pltpu.CompilerParams(vmem_limit_bytes=VMEM_LIMIT),
        cost_estimate=pl.CostEstimate(flops=parts.size, bytes_accessed=2 * parts.size, transcendentals=0),
    )(parts)


def shards(queries, context, vis_blocks, vis_count, w_out, grad_out):
    tokens, width = queries.shape[1:]
    ctx = context.shape[2]
    heads = width // HD
    model = grad_out.shape[2]
    ny, nz = (lax.axis_size(a) for a in DP)
    rows = w_out.shape[1]
    hbm = pl.BlockSpec(memory_space=pltpu.HBM)
    anywhere = pl.BlockSpec(memory_space=pl.ANY)
    vmem = pl.BlockSpec(memory_space=pltpu.VMEM)
    params = pltpu.CompilerParams(vmem_limit_bytes=VMEM_LIMIT)
    small = [
        pltpu.SMEM(vis_blocks.shape, jnp.int32),
        pltpu.SMEM(vis_count.shape, jnp.int32),
        pltpu.VMEM(queries.shape, jnp.bfloat16),
        pltpu.VMEM(context.shape, jnp.bfloat16),
        pltpu.VMEM(grad_out.shape, jnp.bfloat16),
    ]

    used = from_behind(context, "segment", 1)
    near = swap(jnp.broadcast_to(w_out, (nz, rows, width)), True)
    used, _ = lax.optimization_barrier((used, near))
    fixed = [pltpu.with_memory_space_constraint(a, pltpu.HBM) for a in (vis_blocks, vis_count, queries)]
    cotan = pltpu.with_memory_space_constraint(grad_out, pltpu.HBM)

    part = pl.pallas_call(
        forward_kernel,
        name="forward",
        out_shape=jax.ShapeDtypeStruct((nz, ny, rows, width), jnp.bfloat16),
        in_specs=[hbm, hbm, hbm, anywhere, hbm],
        out_specs=vmem,
        scratch_shapes=small + [pltpu.VMEM((tokens, width), jnp.bfloat16), pltpu.SemaphoreType.DMA((5,))],
        compiler_params=params,
        cost_estimate=pl.CostEstimate(
            flops=2 * tokens * width * (2 * ctx + model), bytes_accessed=3 << 20, transcendentals=heads * tokens * ctx
        ),
    )(*fixed, used, cotan)

    once = fold(swap(part, True), jnp.bfloat16)
    grad_weight = fold(swap(once, False), jnp.float32)[None]

    far = swap(jnp.broadcast_to(near[None], (ny, nz, rows, width)), False)
    grad_q, grad_used = pl.pallas_call(
        backward_kernel,
        name="backward",
        out_shape=(
            jax.ShapeDtypeStruct(queries.shape, jnp.bfloat16),
            jax.ShapeDtypeStruct(context.shape, jnp.bfloat16),
        ),
        in_specs=[hbm, hbm, hbm, anywhere, hbm] + [anywhere],
        out_specs=(vmem, vmem),
        scratch_shapes=small
        + [
            pltpu.VMEM((ny, nz, rows, width), jnp.bfloat16),
            pltpu.SemaphoreType.DMA((5,)),
            pltpu.SemaphoreType.DMA((ny,)),
        ],
        compiler_params=params,
        cost_estimate=pl.CostEstimate(
            flops=2 * tokens * width * (6 * ctx + model), bytes_accessed=4 << 20, transcendentals=heads * tokens * ctx
        ),
    )(*fixed, used, cotan, far)
    grad_context = from_behind(grad_used, "segment", -1)
    return grad_q, grad_context, grad_weight


def solution(mesh):
    fine = Mesh(mesh.devices.reshape(4, 8, 8, 4), ("segment", "y", "z", "tensor"))
    in_specs = (
        P("segment", DP, "tensor"),
        P("segment", None, DP, "tensor"),
        P("segment", DP, None),
        P("segment", DP),
        P("segment", DP, "tensor"),
        P("segment", DP, None),
    )
    out_specs = (
        P("segment", DP, "tensor"),
        P("segment", None, DP, "tensor"),
        P("segment", DP, "tensor"),
    )
    return jax.shard_map(shards, mesh=fine, in_specs=in_specs, out_specs=out_specs, check_vma=False)
```
